512 devices in a mesh: tile: 64 (over x, z), dp: 8 (over y, core).
Axes of the slice: x: 4, y: 4, z: 16, core: 2. Of those that a mesh axis runs over, the one named last changes fastest.
Arguments:
- feature_map: bfloat16 [8, 1024, 64, 256], P('dp', 'tile'), may hold values from -16 to 16
- weight: bfloat16 [9, 256, 256], replicated, may hold values from -0.125 to 0.125
- mask_grad: bfloat16 [8, 64, 2, 14, 14, 256], P('dp', 'tile'), may hold values from -6 to 6
- send_count: int32 [8, 64, 8], P('dp', 'tile'), may hold values from 0 to 2, as said below
- send_row: int32 [8, 64, 8, 2], P('dp', 'tile'), may hold values from 0 to 15
- send_col: int32 [8, 64, 8, 2], P('dp', 'tile'), may hold values from 0 to 50
Outputs:
- map_grad: float32 [8, 1024, 64, 256], P('dp', 'tile')
- weight_grad: float32 [9, 256, 256], replicated
The draws below stay inside these ranges and needn't reach their ends.
Inputs may be any that keep to these rules, and one draw needn't show every extreme that they name: `send_count`: in every tile column each head receives exactly 2 live slots in all; one owner image sends 2 * 2 crops in all, one sends none, every other one 2, which is which drawn for each column; in every column some count equals 2.
All inputs are finite; a program needn't handle non-finite values.
Results may differ from the reference program's by a relative error of at most 0.004.
Values may be sent and summed in bfloat16 or wider, within the bound.
No kernel may reach another device: no remote copies, remote signals or barrier semaphores. Data moves between devices by JAX's collectives and lax.ppermute only.
A program may use at most 64 MiB of HBM per device.

```python
import jax
import jax.numpy as jnp
from jax import lax

C = 256
CROP = 14
TH = 16
TW = 64
BOX_DEV = 2
IMAGES = 8
TILES = 64
MAPH = 1024
CAP = 2


def draw_send_count(key, part):
    keys = jax.random.split(key, TILES)
    spread = max(IMAGES - 2, 1)

    def column(column_key):
        key_rank, key_place = jax.random.split(column_key)
        ranking = jax.random.permutation(key_rank, IMAGES)
        placing = jax.random.permutation(key_place, IMAGES)
        order = jnp.arange(IMAGES, dtype=jnp.int32)
        heavy = jnp.clip(2 * BOX_DEV - CAP * order, 0, CAP)
        lighter = BOX_DEV - heavy
        before = jnp.cumsum(lighter) - lighter
        upper = before + lighter
        lanes = order[:, None] - 2
        light_count = (upper[None, :] - lanes + spread - 1) // spread - (before[None, :] - lanes + spread - 1) // spread
        table = jnp.where(order[:, None] == 0, heavy[None, :], jnp.where(order[:, None] == 1, 0, light_count))
        return table[ranking][:, placing]
    tables = jax.vmap(column)(keys)
    return jnp.transpose(tables, (1, 0, 2)).astype(jnp.int32)


def place_ends(result, own_key, low, largest):
    index_at = [jax.random.randint(jax.random.fold_in(own_key, axis), (), 0, length) for axis, length in enumerate(result.shape)]
    longest = result.shape.index(max(result.shape))
    beside = index_at[:longest] + [(index_at[longest] + 1) % result.shape[longest]] + index_at[longest + 1:]
    return result.at[tuple(index_at)].set(low).at[tuple(beside)].set(largest)


def strengthened(drawn, own_key, source, target, parts, factor):
    owner, partner = [(jnp.arange(drawn.shape[axis_at]) // (drawn.shape[axis_at] // parts)).reshape([-1 if axis == axis_at else 1 for axis in range(drawn.ndim)]) for axis_at in (source, target)]
    chosen = jax.random.permutation(own_key, parts)[partner]
    strong = (owner == chosen) | (owner == (partner + parts // 2) % parts)
    return jnp.where(strong, factor * drawn, drawn)


def block_levels(own_key, shape, cuts, least, top_value):
    loudness = 1.0
    for position, shards_of in cuts:
        steps = jax.random.uniform(jax.random.fold_in(jax.random.fold_in(own_key, 6), position), (shards_of,), jnp.float32, least / len(cuts), top_value / len(cuts))
        loudness = loudness * jnp.repeat(jnp.exp(steps), shape[position] // shards_of).reshape((-1,) + (1,) * (len(shape) - 1 - position))
    return loudness


def scatter_about(stream_key, shape, scale, bound, cuts=(), held_as=jnp.bfloat16):
    values = jax.random.normal(stream_key, shape, jnp.float32) * scale
    if len(cuts) > 0:
        values = block_levels(stream_key, shape, cuts, -0.22, 0.18) * values
    return jnp.clip(values, min=-bound, max=bound).astype(held_as)


def heavy_noise(rng, extent, scale, reach, shards, heavy, kind=jnp.bfloat16):
    drawn = scale * jax.random.normal(rng, extent, jnp.float32)
    if shards:
        drawn = drawn * block_levels(rng, extent, shards, -0.22, 0.18)
    return jnp.clip(strengthened(drawn, jax.random.fold_in(rng, 3), *heavy), -reach, reach).astype(kind)


def setup_inputs(seed: int = 0) -> dict:
    key_of = jax.random.split(jax.random.key(seed), 7)
    return {
        "feature_map": heavy_noise(key_of[0], (IMAGES, MAPH, TW, C), 1.0, 16.0, ((0, 8), (1, 64)), (1, 3, 64, 4.0)),
        "weight": scatter_about(key_of[1], (9, C, C), (9 * C) ** -0.5, 0.125),
        "mask_grad": scatter_about(key_of[2], (IMAGES, TILES, BOX_DEV, CROP, CROP, C), 1.0, 6.0, ((0, 8), (1, 64))),
        "send_count": draw_send_count(jax.random.fold_in(key_of[6], 71), 0),
        "send_row": place_ends(jax.random.randint(key_of[4], (IMAGES, TILES, IMAGES, CAP), 0, TH), jax.random.fold_in(key_of[4], 1), 0, TH - 1).astype(jnp.int32),
        "send_col": place_ends(jax.random.randint(key_of[5], (IMAGES, TILES, IMAGES, CAP), 0, TW - CROP + 1), jax.random.fold_in(key_of[5], 1), 0, TW - CROP).astype(jnp.int32),
    }


GELU_SCALE = 0.7978845608
GELU_CUBIC = 0.044715


def gelu_slope(values):
    inner = GELU_SCALE * (values + GELU_CUBIC * values * values * values)
    tangent = jnp.tanh(inner)
    outer = 0.5 * values * (1.0 - tangent * tangent) * GELU_SCALE * (1.0 + 3.0 * GELU_CUBIC * values * values)
    return 0.5 * (1.0 + tangent) + outer


def conv_backward(crops, weight, upstream):
    box_count = crops.shape[0]
    crop_side = crops.shape[1]
    channels = crops.shape[3]
    padded = jnp.pad(crops, ((0, 0), (1, 1), (1, 1), (0, 0)))
    windows = []
    for tap_index in range(9):
        tap_row = tap_index // 3
        tap_col = tap_index % 3
        windows.append(padded[:, tap_row:tap_row + crop_side, tap_col:tap_col + crop_side, :].reshape(-1, channels))
    pre_act = jnp.zeros((windows[0].shape[0], weight.shape[2]), jnp.float32)
    for tap_index in range(9):
        pre_act = pre_act + jnp.dot(windows[tap_index], weight[tap_index], preferred_element_type=jnp.float32)
    slope = (upstream.reshape(pre_act.shape).astype(jnp.float32) * gelu_slope(pre_act)).astype(jnp.bfloat16)
    weight_list = []
    for tap_index in range(9):
        weight_list.append(lax.dot_general(windows[tap_index], slope, (((0,), (0,)), ((), ())), preferred_element_type=jnp.float32))
    weight_terms = jnp.stack(weight_list)
    grad_pad = jnp.zeros((box_count, crop_side + 2, crop_side + 2, channels), jnp.float32)
    for tap_index in range(9):
        tap_row = tap_index // 3
        tap_col = tap_index % 3
        part_grad = lax.dot_general(slope, weight[tap_index], (((1,), (1,)), ((), ())), preferred_element_type=jnp.float32)
        grad_pad = grad_pad.at[:, tap_row:tap_row + crop_side, tap_col:tap_col + crop_side, :].add(part_grad.reshape(box_count, crop_side, crop_side, channels))
    crop_grad = grad_pad[:, 1:crop_side + 1, 1:crop_side + 1, :].astype(jnp.bfloat16)
    return weight_terms, crop_grad


def selector(live, slot_total):
    ranks = jnp.cumsum(live) - 1
    targets = lax.broadcasted_iota(jnp.int32, (slot_total, live.shape[0]), 0)
    chosen = (ranks[None, :] == targets) & (live[None, :] > 0)
    return chosen.astype(jnp.bfloat16)


def cut_crops(extended, top_rows, left_cols, crop_side):
    def single(top_row, left_col):
        return lax.dynamic_slice(extended, (top_row, left_col, top_row * 0), (crop_side, crop_side, extended.shape[2]))
    return jax.vmap(single)(top_rows, left_cols)


def add_crops(canvas, pieces, top_rows, left_cols, live):
    crop_side = pieces.shape[1]
    channels = canvas.shape[2]

    def place(slot_index, running):
        anchor = (top_rows[slot_index], left_cols[slot_index], top_rows[slot_index] * 0)
        current = lax.dynamic_slice(running, anchor, (crop_side, crop_side, channels))
        update = current + pieces[slot_index].astype(running.dtype) * live[slot_index]
        return lax.dynamic_update_slice(running, update, anchor)
    return lax.fori_loop(0, pieces.shape[0], place, canvas)


def reference(feature_map, weight, mask_grad, send_count, send_row, send_col):
    images = feature_map.shape[0]
    map_width = feature_map.shape[2]
    channels = feature_map.shape[3]
    tiles = send_count.shape[1]
    tile_height = feature_map.shape[1] // tiles
    boxes_head = mask_grad.shape[2]
    crop_side = mask_grad.shape[3]
    halo_rows = crop_side - 1
    slot_cap = send_row.shape[3]
    padded_map = jnp.concatenate([feature_map, jnp.zeros((images, halo_rows, map_width, channels), jnp.bfloat16)], 1)
    slot_iota = lax.broadcasted_iota(jnp.int32, (images, images, slot_cap), 2)

    def cutter(extended, top_rows, left_cols):
        return cut_crops(extended, top_rows, left_cols, crop_side)

    def column(carry, tile_id):
        spill, weight_total = carry
        extended = lax.dynamic_slice_in_dim(padded_map, tile_id * tile_height, tile_height + halo_rows, 1)
        top_rows = lax.dynamic_index_in_dim(send_row, tile_id, 1, keepdims=False).reshape(images, -1)
        left_cols = lax.dynamic_index_in_dim(send_col, tile_id, 1, keepdims=False).reshape(images, -1)
        counts = lax.dynamic_index_in_dim(send_count, tile_id, 1, keepdims=False)
        live = (slot_iota < counts[:, :, None]).astype(jnp.int32)
        crops = jax.vmap(cutter)(extended, top_rows, left_cols).reshape(images, images, slot_cap, -1)
        pickers = []
        head_boxes = []
        for head in range(images):
            picker = selector(live[:, head].reshape(-1), boxes_head)
            pickers.append(picker)
            flat = crops[:, head].reshape(images * slot_cap, -1)
            head_boxes.append(jnp.dot(picker, flat, preferred_element_type=jnp.float32).astype(jnp.bfloat16))
        all_boxes = jnp.concatenate(head_boxes, 0).reshape(images * boxes_head, crop_side, crop_side, channels)
        upstream = lax.dynamic_index_in_dim(mask_grad, tile_id, 1, keepdims=False).reshape(images * boxes_head, crop_side, crop_side, channels)
        weight_terms, crop_grad = conv_backward(all_boxes, weight, upstream)
        crop_flat = crop_grad.reshape(images, boxes_head, -1)
        slot_list = []
        for head in range(images):
            back = jnp.dot(pickers[head].T, crop_flat[head], preferred_element_type=jnp.float32).astype(jnp.bfloat16)
            slot_list.append(back.reshape(images, slot_cap, -1))
        slot_grads = jnp.stack(slot_list, 1).reshape(images, images * slot_cap, crop_side, crop_side, channels)
        canvas = jnp.zeros((images, tile_height + halo_rows, map_width, channels), jnp.float32)
        canvas = jax.vmap(add_crops)(canvas, slot_grads, top_rows, left_cols, live.reshape(images, -1).astype(jnp.float32))
        main = jnp.concatenate([canvas[:, :halo_rows] + spill, canvas[:, halo_rows:tile_height]], 1)
        return (canvas[:, tile_height:], weight_total + weight_terms), main

    start_spill = jnp.zeros((images, halo_rows, map_width, channels), jnp.float32)
    start_weight = jnp.zeros(weight.shape, jnp.float32)
    final, mains = lax.scan(column, (start_spill, start_weight), jnp.arange(tiles, dtype=jnp.int32))
    map_grad = jnp.transpose(mains, (1, 0, 2, 3, 4)).reshape(images, tiles * tile_height, map_width, channels)
    weight_grad = final[1] / (images * tiles * boxes_head)
    return map_grad, weight_grad
```

```python
import jax
import jax.numpy as jnp
from jax import lax
from jax.experimental import pallas as pl
from jax.experimental.pallas import tpu as pltpu
from jax.sharding import PartitionSpec as P

GELU_SCALE = 0.7978845608
GELU_CUBIC = 0.044715
F32 = jnp.float32
BF16 = jnp.bfloat16
XP = 16
LEFT = 8


def gelu_slope(values):
    inner = GELU_SCALE * (values + GELU_CUBIC * values * values * values)
    tangent = jnp.tanh(inner)
    outer = (
        0.5
        * values
        * (1.0 - tangent * tangent)
        * GELU_SCALE
        * (1.0 + 3.0 * GELU_CUBIC * values * values)
    )
    return 0.5 * (1.0 + tangent) + outer


def column_iota(rows):
    flat = lax.broadcasted_iota(jnp.int32, (rows, 1), 0)
    return lax.rem(flat, XP)


def forward_kernel(dims, me_ref, counts_ref, own_ref, row_ref, col_ref, map_ref, halo_ref, up_ref, weight_ref,
                   wgrad_ref, slope_ref, wide, shifted, slid, slot):
    side, slots, heads, cap, owners = dims
    high = map_ref.shape[0]
    halo = halo_ref.shape[0]
    width = map_ref.shape[1]
    channels = map_ref.shape[2]
    area = side * XP
    padded = (side + 2) * XP
    me = me_ref[0]

    for index in range(slots):
        for field in range(4):
            slot[field, index] = 0

    def head(j, used):
        before = lax.fori_loop(0, me, lambda i, total: total + counts_ref[i, j], 0)
        count = own_ref[j]
        for r in range(cap):
            live = (r < count) & (used < slots)

            @pl.when(live)
            def _():
                slot[0, used] = j
                slot[1, used] = before + r
                slot[2, used] = row_ref[j, r]
                slot[3, used] = col_ref[j, r]

            used = used + live.astype(jnp.int32)
        return used

    used = lax.fori_loop(0, heads, head, 0)

    wide[pl.ds(0, high), pl.ds(LEFT, width), :] = map_ref[...].astype(F32)
    wide[pl.ds(high, halo), pl.ds(LEFT, width), :] = halo_ref[...].astype(F32)

    columns = lax.broadcasted_iota(jnp.int32, (side, XP, channels), 1)
    flat_columns = lax.broadcasted_iota(jnp.int32, (side, XP, channels), 1).reshape(area, channels)
    none = jnp.zeros((XP, channels), BF16)
    for s in range(slots):
        live = s < used
        top = slot[2, s]
        left = slot[3, s]
        base = pl.multiple_of(left // 8 * 8, 8)
        window_all = wide[pl.ds(top, side), pl.ds(base, 2 * XP), :]
        window_all = pltpu.roll(window_all, 2 * XP - (LEFT - 1) - lax.rem(left, 8), 1)
        for b in range(3):
            window = (window_all if b == 0 else pltpu.roll(window_all, 2 * XP - b, 1))[:, :XP]
            low = jnp.where(live, max(0, 1 - b), XP)
            keep = (columns >= low) & (columns < min(side, side + 1 - b))
            shifted[b, pl.ds(s * padded, XP), :] = none
            shifted[b, pl.ds(s * padded + XP, area), :] = (
                jnp.where(keep, window, 0.0).astype(BF16).reshape(area, channels)
            )
            shifted[b, pl.ds(s * padded + XP + area, XP), :] = none

    for s in range(slots):
        taps = [
            shifted[b, pl.ds(s * padded + a * XP, area), :] for a in range(3) for b in range(3)
        ]
        lhs = jnp.concatenate(taps, axis=1)
        pre = jnp.dot(lhs, weight_ref[...].reshape(9 * channels, channels), preferred_element_type=F32)
        upstream = up_ref[slot[0, s], slot[1, s]].astype(F32).reshape(area, channels)
        last = jnp.where(s < used, side, 0)
        slope = jnp.where(flat_columns < last, upstream * gelu_slope(pre), 0.0).astype(BF16)
        slope_ref[pl.ds(s * area, area), :] = slope
        for a in range(3):
            if a > 0:
                slid[a, pl.ds(s * padded, a * XP), :] = jnp.zeros((a * XP, channels), BF16)
            slid[a, pl.ds(s * padded + a * XP, area), :] = slope
            if a < 2:
                slid[a, pl.ds(s * padded + a * XP + area, (2 - a) * XP), :] = jnp.zeros(
                    ((2 - a) * XP, channels), BF16
                )

    half = channels // 2
    rows = channels // 8
    for b in range(3):
        rhs = jnp.concatenate([slid[a] for a in range(3)], axis=1)
        terms = lax.dot_general(
            shifted[b], rhs, (((0,), (0,)), ((), ())), preferred_element_type=F32
        )
        for a in range(3):
            for part in range(2):
                piece = terms[:, a * channels + part * half : a * channels + (part + 1) * half]
                wgrad_ref[pl.ds((3 * a + b) * rows, rows), part] = piece.reshape(rows, 8, half)


def backward_kernel(dims, own_ref, row_ref, col_ref, slope_ref, weight_ref, main_ref, spill_ref, canvas, shifted,
                    slot):
    side, slots, heads, cap, owners = dims
    high = main_ref.shape[0]
    width = main_ref.shape[1]
    channels = main_ref.shape[2]
    halo = spill_ref.shape[0]
    area = side * XP
    padded = (side + 2) * XP

    for index in range(slots):
        for field in range(2):
            slot[field, index] = 0

    def head(j, used):
        count = own_ref[j]
        for r in range(cap):
            live = (r < count) & (used < slots)

            @pl.when(live)
            def _():
                slot[0, used] = row_ref[j, r]
                slot[1, used] = col_ref[j, r]

            used = used + live.astype(jnp.int32)
        return used

    used = lax.fori_loop(0, heads, head, 0)

    canvas[...] = jnp.zeros(canvas.shape, F32)
    none = jnp.zeros((XP, channels), BF16)
    rhs = jnp.concatenate([weight_ref[k] for k in range(9)], axis=1)
    columns = lax.broadcasted_iota(jnp.int32, (side, XP, channels), 1)
    for s in range(slots):
        slope = slope_ref[pl.ds(s * area, area), :].astype(F32)
        for b in range(3):
            moved = slope if b == 1 else pltpu.roll(slope, (area + b - 1) % area, 0)
            shifted[b, pl.ds(0, XP), :] = none
            shifted[b, pl.ds(XP, area), :] = moved.astype(BF16)
            shifted[b, pl.ds(XP + area, XP), :] = none
        taps = [shifted[b, pl.ds((2 - a) * XP, area), :] for a in range(3) for b in range(3)]
        lhs = jnp.concatenate(taps, axis=1)
        grad = lax.dot_general(lhs, rhs, (((1,), (1,)), ((), ())), preferred_element_type=F32)
        grad = grad.astype(BF16).astype(F32).reshape(side, XP, channels)
        last = jnp.where(s < used, side, 0)
        grad = jnp.where(columns < last, grad, 0.0)
        left = slot[1, s]
        grad = jnp.concatenate([grad, jnp.zeros((side, XP // 2, channels), F32)], axis=1)
        grad = pltpu.roll(grad, lax.rem(left, 8), 1)
        base = pl.multiple_of(left // 8 * 8, 8)
        place = (pl.ds(slot[0, s], side), pl.ds(base, XP + XP // 2), slice(None))
        canvas[place] = canvas[place] + grad
    main_ref[...] = canvas[pl.ds(0, high), pl.ds(0, width), :]
    spill_ref[...] = canvas[pl.ds(high, halo), pl.ds(0, width), :].astype(spill_ref.dtype)


def finish_kernel(core_ref, mine_ref, other_ref, out_ref):
    rows = mine_ref.shape[0] // 16
    half = out_ref.shape[0] // 2
    lanes = mine_ref.shape[1]
    core = core_ref[0]
    for part in range(2):
        source = jnp.where(core == part, mine_ref[...], other_ref[...]).astype(F32)
        source = source.reshape(rows, 2, 8, lanes)
        for piece in range(2):
            out_ref[pl.ds(part * half, half), pl.ds(piece * lanes, lanes)] = source[:, piece].reshape(half, lanes)


def smem():
    return pl.BlockSpec(memory_space=pltpu.SMEM)


def vmem():
    return pl.BlockSpec(memory_space=pltpu.VMEM)


def shift(array, axis, by):
    length = lax.axis_size(axis)
    pairs = [(i, i + by) for i in range(length) if 0 <= i + by < length]
    return lax.ppermute(array, axis, pairs)


def repeated(array, times):
    return jnp.broadcast_to(array[None], (times,) + array.shape)


def on_device(feature_map, weight, mask_grad, send_count, send_row, send_col):
    tile_map = feature_map[0]
    high, width, channels = tile_map.shape
    boxes, side = mask_grad.shape[2], mask_grad.shape[3]
    heads, cap = send_row.shape[2], send_row.shape[3]
    owners = lax.axis_size("dp")
    tiles = lax.axis_size("tile")
    slots = boxes * cap
    halo = side - 1
    area, padded = side * XP, (side + 2) * XP
    dims = (side, slots, heads, cap, owners)
    me = lax.axis_index("dp")
    me_array = me.reshape(1).astype(jnp.int32)
    own, top_rows, left_cols = send_count[0, 0], send_row[0, 0], send_col[0, 0]

    below = shift(tile_map[:halo], "tile", -1)
    counts = lax.all_to_all(repeated(own, owners), "dp", 0, 0, tiled=True)
    up = jnp.pad(mask_grad[0, 0], ((0, 0), (0, 0), (0, XP - side), (0, 0)))
    ups = lax.all_to_all(repeated(up, owners), "dp", 0, 0, tiled=True)

    wgrad, slope = pl.pallas_call(
        lambda *refs: forward_kernel(dims, *refs),
        out_shape=(
            jax.ShapeDtypeStruct((9 * channels // 8, 2, 8, channels // 2), F32),
            jax.ShapeDtypeStruct((slots * area, channels), BF16),
        ),
        in_specs=[smem()] * 5 + [vmem()] * 4,
        out_specs=(vmem(), vmem()),
        scratch_shapes=[
            pltpu.VMEM((high + halo, width + 2 * LEFT, channels), F32),
            pltpu.VMEM((3, slots * padded, channels), BF16),
            pltpu.VMEM((3, slots * padded, channels), BF16),
            pltpu.SMEM((4, slots), jnp.int32),
        ],
        name="forward",
    )(me_array, counts, own, top_rows, left_cols, tile_map, below, ups, weight)

    main, spill = pl.pallas_call(
        lambda *refs: backward_kernel(dims, *refs),
        out_shape=(
            jax.ShapeDtypeStruct((high, width, channels), F32),
            jax.ShapeDtypeStruct((halo, width, channels), BF16),
        ),
        in_specs=[smem()] * 3 + [vmem()] * 2,
        out_specs=(vmem(), vmem()),
        scratch_shapes=[
            pltpu.VMEM((high + halo, width + XP, channels), F32),
            pltpu.VMEM((3, padded, channels), BF16),
            pltpu.SMEM((2, slots), jnp.int32),
        ],
        name="backward",
    )(own, top_rows, left_cols, slope, weight)
    arriving = shift(spill, "tile", 1).astype(F32)
    map_grad = jnp.concatenate([main[:halo] + arriving, main[halo:]], 0)

    core = lax.rem(me, 2)
    partner = [(i, i ^ 1) for i in range(owners)]
    chips = owners // 2
    same_core = [[2 * i + c for i in range(chips)] for c in range(2)]
    lanes = channels // 2
    total = 9 * channels * 2
    halves = wgrad.reshape(2, total // 2, lanes)
    mine = jnp.where(core == 0, halves[0], halves[1])
    theirs = jnp.where(core == 0, halves[1], halves[0])
    pair = (mine + lax.ppermute(theirs, "dp", partner)).astype(BF16)
    quarter = total // 2 // chips
    got = lax.all_to_all(
        pair.reshape(chips, quarter, lanes), "dp", 0, 0, axis_index_groups=same_core, tiled=True
    )
    column = got.astype(F32).sum(0)
    got = lax.all_to_all(column.reshape(tiles, quarter // tiles, lanes), "tile", 0, 0, tiled=True)
    chunk = (got.sum(0) / (boxes * tiles * owners)).astype(BF16)
    got = lax.all_to_all(repeated(chunk, tiles), "tile", 0, 0, tiled=True).reshape(quarter, lanes)
    got = lax.all_to_all(repeated(got, chips), "dp", 0, 0, axis_index_groups=same_core, tiled=True)
    got = got.reshape(total // 2, lanes)
    other = lax.ppermute(got, "dp", partner)
    weight_grad = pl.pallas_call(
        finish_kernel,
        out_shape=jax.ShapeDtypeStruct((9 * channels, channels), F32),
        in_specs=[smem(), vmem(), vmem()],
        out_specs=vmem(),
        name="finish",
    )(core.reshape(1), got, other)
    return map_grad[None], weight_grad.reshape(9, channels, channels)


def solution(mesh):
    in_specs = (
        P("dp", "tile", None, None),
        P(),
        P("dp", "tile", None, None, None, None),
        P("dp", "tile", None),
        P("dp", "tile", None, None),
        P("dp", "tile", None, None),
    )
    out_specs = (P("dp", "tile", None, None), P())
    return jax.shard_map(
        on_device, mesh=mesh, in_specs=in_specs, out_specs=out_specs, check_vma=False
    )
```

```python
import jax
import jax.numpy as jnp
from jax import lax
from jax.experimental import pallas as pl
from jax.experimental.pallas import tpu as pltpu
from jax.sharding import PartitionSpec as P

GELU_SCALE = 0.7978845608
GELU_CUBIC = 0.044715
F32 = jnp.float32
BF16 = jnp.bfloat16
XP = 16
LEFT = 8


def gelu_slope(values):
    inner = GELU_SCALE * (values + GELU_CUBIC * values * values * values)
    tangent = jnp.tanh(inner)
    outer = (
        0.5
        * values
        * (1.0 - tangent * tangent)
        * GELU_SCALE
        * (1.0 + 3.0 * GELU_CUBIC * values * values)
    )
    return 0.5 * (1.0 + tangent) + outer


def forward_kernel(dims, own_ref, row_ref, col_ref, map_ref, halo_ref, weight_ref,
                   gelu_ref, shifted, wide, slot):
    side, slots, heads, cap = dims
    high = map_ref.shape[0]
    halo = halo_ref.shape[0]
    width = map_ref.shape[1]
    channels = map_ref.shape[2]
    area = side * XP
    padded = (side + 2) * XP
    used = list_slots(dims, own_ref, slot, lambda j, r: (row_ref[j, r], col_ref[j, r]))

    wide[pl.ds(0, high), pl.ds(LEFT, width), :] = map_ref[...].astype(F32)
    wide[pl.ds(high, halo), pl.ds(LEFT, width), :] = halo_ref[...].astype(F32)

    columns = lax.broadcasted_iota(jnp.int32, (side, XP, channels), 1)
    none = jnp.zeros((XP, channels), BF16)
    for s in range(slots):
        live = s < used
        top = slot[0, s]
        left = slot[1, s]
        base = pl.multiple_of(left // 8 * 8, 8)
        window_all = wide[pl.ds(top, side), pl.ds(base, 2 * XP), :]
        window_all = pltpu.roll(window_all, 2 * XP - (LEFT - 1) - lax.rem(left, 8), 1)
        for b in range(3):
            window = (window_all if b == 0 else pltpu.roll(window_all, 2 * XP - b, 1))[:, :XP]
            low = jnp.where(live, max(0, 1 - b), XP)
            keep = (columns >= low) & (columns < min(side, side + 1 - b))
            shifted[b, pl.ds(s * padded, XP), :] = none
            shifted[b, pl.ds(s * padded + XP, area), :] = (
                jnp.where(keep, window, 0.0).astype(BF16).reshape(area, channels)
            )
            shifted[b, pl.ds(s * padded + XP + area, XP), :] = none

    for s in range(slots):
        taps = [
            shifted[b, pl.ds(s * padded + a * XP, area), :] for a in range(3) for b in range(3)
        ]
        lhs = jnp.concatenate(taps, axis=1)
        pre = jnp.dot(lhs, weight_ref[...].reshape(9 * channels, channels), preferred_element_type=F32)
        gelu_ref[pl.ds(s * area, area), :] = gelu_slope(pre)


def list_slots(dims, own_ref, slot, fields):
    side, slots, heads, cap = dims
    width = slot.shape[0]
    for index in range(slots):
        for field in range(width):
            slot[field, index] = 0

    def head(j, used):
        count = own_ref[j]
        for r in range(cap):
            live = (r < count) & (used < slots)

            @pl.when(live)
            def _():
                for field, value in enumerate(fields(j, r)):
                    slot[field, used] = value

            used = used + live.astype(jnp.int32)
        return used

    return lax.fori_loop(0, heads, head, 0)


def slope_kernel(dims, me_ref, own_ref, ours_ref, across_ref, gelu_ref, shifted, mine_ref, theirs_ref, slope_ref,
                 slid, prior, slot):
    side, slots, heads, cap = dims
    boxes = ours_ref.shape[1]
    channels = gelu_ref.shape[1]
    area = side * XP
    padded = (side + 2) * XP
    me = me_ref[0]
    core = lax.rem(me, 2)

    lane = lax.broadcasted_iota(jnp.int32, (8, channels), 1)
    totals = jnp.zeros((8, channels), F32)
    for i in range(heads):
        row = jnp.where(core == i % 2, ours_ref[i // 2, 0, 0], across_ref[i // 2, 0, 0]).astype(F32)[8:16]
        totals = totals + jnp.where(i < me, row, 0.0)
    line = lax.broadcasted_iota(jnp.int32, (8, channels), 0)
    totals = jnp.where(line == side - 8, totals, 0.0)
    for j in range(heads):
        prior[j] = jnp.sum(jnp.where(lane == j, totals, 0.0)).astype(jnp.int32)
    used = list_slots(dims, own_ref, slot, lambda j, r: (j, jnp.minimum(prior[j] + r, boxes - 1)))

    flat_columns = lax.broadcasted_iota(jnp.int32, (side, XP, channels), 1).reshape(area, channels)
    for s in range(slots):
        chip = slot[0, s] // 2
        box = slot[1, s]
        same = lax.rem(slot[0, s], 2) == core
        upstream = jnp.where(same, ours_ref[chip, box].astype(F32), across_ref[chip, box].astype(F32))
        upstream = upstream.reshape(area, channels)
        last = jnp.where(s < used, side, 0)
        slope = upstream * gelu_ref[pl.ds(s * area, area), :]
        slope = jnp.where(flat_columns < last, slope, 0.0).astype(BF16)
        slope_ref[pl.ds(s * area, area), :] = slope
        for a in range(3):
            if a > 0:
                slid[a, pl.ds(s * padded, a * XP), :] = jnp.zeros((a * XP, channels), BF16)
            slid[a, pl.ds(s * padded + a * XP, area), :] = slope
            if a < 2:
                slid[a, pl.ds(s * padded + a * XP + area, (2 - a) * XP), :] = jnp.zeros(
                    ((2 - a) * XP, channels), BF16
                )

    half = channels // 2
    rows = channels // 8
    split = 9 * rows // 2
    for b in range(3):
        rhs = jnp.concatenate([slid[a] for a in range(3)], axis=1)
        terms = lax.dot_general(
            shifted[b], rhs, (((0,), (0,)), ((), ())), preferred_element_type=F32
        )
        for a in range(3):
            first = (3 * a + b) * rows
            for low, end, part in ((first, min(first + rows, split), 0), (max(first, split), first + rows, 1)):
                if low >= end:
                    continue
                pieces = [
                    terms[
                        (low - first) * 8 : (end - first) * 8,
                        a * channels + side_ * half : a * channels + (side_ + 1) * half,
                    ].reshape(end - low, 8, half)
                    for side_ in range(2)
                ]
                for ref, wanted in ((mine_ref, part), (theirs_ref, 1 - part)):

                    @pl.when(core == wanted)
                    def _():
                        for side_ in range(2):
                            ref[pl.ds(low - part * split, end - low), side_] = pieces[side_]


def backward_kernel(dims, own_ref, row_ref, col_ref, slope_ref, weight_ref, main_ref, spill_ref, canvas, shifted,
                    slot):
    side, slots, heads, cap = dims
    high = main_ref.shape[0]
    width = main_ref.shape[1]
    channels = main_ref.shape[2]
    halo = spill_ref.shape[0]
    area = side * XP
    padded = (side + 2) * XP

    used = list_slots(dims, own_ref, slot, lambda j, r: (row_ref[j, r], col_ref[j, r]))
    canvas[...] = jnp.zeros(canvas.shape, F32)
    none = jnp.zeros((XP, channels), BF16)
    rhs = jnp.concatenate([weight_ref[k] for k in range(9)], axis=1)
    columns = lax.broadcasted_iota(jnp.int32, (side, XP, channels), 1)
    for s in range(slots):
        slope = slope_ref[pl.ds(s * area, area), :].astype(F32)
        for b in range(3):
            moved = slope if b == 1 else pltpu.roll(slope, (area + b - 1) % area, 0)
            shifted[b, pl.ds(0, XP), :] = none
            shifted[b, pl.ds(XP, area), :] = moved.astype(BF16)
            shifted[b, pl.ds(XP + area, XP), :] = none
        taps = [shifted[b, pl.ds((2 - a) * XP, area), :] for a in range(3) for b in range(3)]
        lhs = jnp.concatenate(taps, axis=1)
        grad = lax.dot_general(lhs, rhs, (((1,), (1,)), ((), ())), preferred_element_type=F32)
        grad = grad.astype(BF16).astype(F32).reshape(side, XP, channels)
        last = jnp.where(s < used, side, 0)
        grad = jnp.where(columns < last, grad, 0.0)
        left = slot[1, s]
        grad = jnp.concatenate([grad, jnp.zeros((side, XP // 2, channels), F32)], axis=1)
        grad = pltpu.roll(grad, lax.rem(left, 8), 1)
        base = pl.multiple_of(left // 8 * 8, 8)
        place = (pl.ds(slot[0, s], side), pl.ds(base, XP + XP // 2), slice(None))
        canvas[place] = canvas[place] + grad
    main_ref[...] = canvas[pl.ds(0, high), pl.ds(0, width), :]
    spill_ref[...] = canvas[pl.ds(high, halo), pl.ds(0, width), :].astype(spill_ref.dtype)


def finish_kernel(core_ref, mine_ref, other_ref, out_ref):
    rows = mine_ref.shape[0] // 16
    half = out_ref.shape[0] // 2
    lanes = mine_ref.shape[1]
    core = core_ref[0]
    for part in range(2):
        source = jnp.where(core == part, mine_ref[...], other_ref[...]).astype(F32)
        source = source.reshape(rows, 2, 8, lanes)
        for piece in range(2):
            out_ref[pl.ds(part * half, half), pl.ds(piece * lanes, lanes)] = source[:, piece].reshape(half, lanes)


def smem():
    return pl.BlockSpec(memory_space=pltpu.SMEM)


def vmem():
    return pl.BlockSpec(memory_space=pltpu.VMEM)


def shift(array, axis, by):
    length = lax.axis_size(axis)
    pairs = [(i, i + by) for i in range(length) if 0 <= i + by < length]
    return lax.ppermute(array, axis, pairs)


def repeated(array, times):
    return jnp.broadcast_to(array[None], (times,) + array.shape)


def on_device(feature_map, weight, mask_grad, send_count, send_row, send_col):
    tile_map = feature_map[0]
    high, width, channels = tile_map.shape
    boxes, side = mask_grad.shape[2], mask_grad.shape[3]
    heads, cap = send_row.shape[2], send_row.shape[3]
    owners = lax.axis_size("dp")
    tiles = lax.axis_size("tile")
    slots = boxes * cap
    halo = side - 1
    area, padded = side * XP, (side + 2) * XP
    dims = (side, slots, heads, cap)
    me = lax.axis_index("dp")
    me_array = me.reshape(1).astype(jnp.int32)
    own, top_rows, left_cols = send_count[0, 0], send_row[0, 0], send_col[0, 0]
    partner = [(i, i ^ 1) for i in range(owners)]
    chips = owners // 2
    same_core = [[2 * i + c for i in range(chips)] for c in range(2)]

    below = shift(tile_map[:halo], "tile", -1)
    spare = jnp.pad(own.astype(BF16), (0, channels - heads))
    spare = jnp.broadcast_to(spare, (boxes, side, XP - side, channels))
    up = jnp.concatenate([mask_grad[0, 0], spare], 2)
    ups = lax.all_to_all(
        repeated(up, chips), "dp", 0, 0, axis_index_groups=same_core, tiled=True
    )
    partner_ups = lax.ppermute(ups, "dp", partner)
    core = lax.rem(me, 2)

    gelu, shifted = pl.pallas_call(
        lambda *refs: forward_kernel(dims, *refs),
        out_shape=(
            jax.ShapeDtypeStruct((slots * area, channels), F32),
            jax.ShapeDtypeStruct((3, slots * padded, channels), BF16),
        ),
        in_specs=[smem()] * 3 + [vmem()] * 3,
        out_specs=(vmem(), vmem()),
        scratch_shapes=[
            pltpu.VMEM((high + halo, width + 2 * LEFT, channels), F32),
            pltpu.SMEM((2, slots), jnp.int32),
        ],
        name="forward",
    )(own, top_rows, left_cols, tile_map, below, weight)

    lanes = channels // 2
    total = 9 * channels * 2
    split = jax.ShapeDtypeStruct((total // 32, 2, 8, lanes), F32)
    mine, theirs, slope = pl.pallas_call(
        lambda *refs: slope_kernel(dims, *refs),
        out_shape=(split, split, jax.ShapeDtypeStruct((slots * area, channels), BF16)),
        in_specs=[smem()] * 2 + [vmem()] * 4,
        out_specs=(vmem(), vmem(), vmem()),
        scratch_shapes=[
            pltpu.VMEM((3, slots * padded, channels), BF16),
            pltpu.SMEM((heads,), jnp.int32),
            pltpu.SMEM((2, slots), jnp.int32),
        ],
        name="slope",
    )(me_array, own, ups, partner_ups, gelu, shifted)

    main, spill = pl.pallas_call(
        lambda *refs: backward_kernel(dims, *refs),
        out_shape=(
            jax.ShapeDtypeStruct((high, width, channels), F32),
            jax.ShapeDtypeStruct((halo, width, channels), BF16),
        ),
        in_specs=[smem()] * 3 + [vmem()] * 2,
        out_specs=(vmem(), vmem()),
        scratch_shapes=[
            pltpu.VMEM((high + halo, width + XP, channels), F32),
            pltpu.VMEM((3, padded, channels), BF16),
            pltpu.SMEM((2, slots), jnp.int32),
        ],
        name="backward",
    )(own, top_rows, left_cols, slope, weight)
    arriving = shift(spill, "tile", 1).astype(F32)
    map_grad = jnp.concatenate([main[:halo] + arriving, main[halo:]], 0)

    part = total // 2
    deep = 16 if tiles % 16 == 0 else 1
    wide = tiles // deep
    plane = [
        [(x * deep + z) * owners + 2 * y + c for x in range(wide) for y in range(chips)]
        for z in range(deep)
        for c in range(2)
    ]
    stick = [[x * deep + z for z in range(deep)] for x in range(wide)]
    near = wide * chips
    pair = (mine.reshape(part, lanes) + lax.ppermute(theirs, "dp", partner).reshape(part, lanes)).astype(BF16)
    got = lax.all_to_all(
        pair.reshape(near, part // near, lanes), ("tile", "dp"), 0, 0, axis_index_groups=plane, tiled=True
    )
    column = got.astype(F32).sum(0)
    got = lax.all_to_all(
        column.reshape(deep, part // near // deep, lanes), "tile", 0, 0, axis_index_groups=stick, tiled=True
    )
    chunk = (got.sum(0) / (boxes * tiles * owners)).astype(BF16)
    got = lax.all_to_all(repeated(chunk, deep), "tile", 0, 0, axis_index_groups=stick, tiled=True)
    got = got.reshape(part // near, lanes)
    got = lax.all_to_all(repeated(got, near), ("tile", "dp"), 0, 0, axis_index_groups=plane, tiled=True)
    got = got.reshape(part, lanes)
    other = lax.ppermute(got, "dp", partner)
    weight_grad = pl.pallas_call(
        finish_kernel,
        out_shape=jax.ShapeDtypeStruct((9 * channels, channels), F32),
        in_specs=[smem(), vmem(), vmem()],
        out_specs=vmem(),
        name="finish",
    )(core.reshape(1), got, other)
    return map_grad[None], weight_grad.reshape(9, channels, channels)


def solution(mesh):
    in_specs = (
        P("dp", "tile", None, None),
        P(),
        P("dp", "tile", None, None, None, None),
        P("dp", "tile", None),
        P("dp", "tile", None, None),
        P("dp", "tile", None, None),
    )
    out_specs = (P("dp", "tile", None, None), P())
    return jax.shard_map(
        on_device, mesh=mesh, in_specs=in_specs, out_specs=out_specs, check_vma=False
    )
```

```python
import jax
import jax.numpy as jnp
from jax import lax
from jax.experimental import pallas as pl
from jax.experimental.pallas import tpu as pltpu
from jax.sharding import PartitionSpec as P


GELU_SCALE = 0.7978845608
GELU_CUBIC = 0.044715
F32 = jnp.float32
BF16 = jnp.bfloat16
VMEM_BYTES = 20 * 2**20
XP = 16
LEFT = 8


def gelu_slope(values):
    inner = GELU_SCALE * (values + GELU_CUBIC * values * values * values)
    tangent = jnp.tanh(inner)
    outer = (
        0.5
        * values
        * (1.0 - tangent * tangent)
        * GELU_SCALE
        * (1.0 + 3.0 * GELU_CUBIC * values * values)
    )
    return 0.5 * (1.0 + tangent) + outer


def forward_kernel(dims, own_ref, row_ref, col_ref, map_ref, halo_ref, weight_ref,
                   gelu_ref, shifted, wide, slot):
    side, slots, _, _ = dims
    high = map_ref.shape[0]
    halo = halo_ref.shape[0]
    width = map_ref.shape[1]
    channels = map_ref.shape[2]
    area = side * XP
    padded = (side + 2) * XP
    used = list_slots(dims, own_ref, slot, lambda j, r: (row_ref[j, r], col_ref[j, r]))

    wide[pl.ds(0, high), pl.ds(LEFT, width), :] = map_ref[...].astype(F32)
    wide[pl.ds(high, halo), pl.ds(LEFT, width), :] = halo_ref[...].astype(F32)

    columns = lax.broadcasted_iota(jnp.int32, (side, XP, channels), 1)
    none = jnp.zeros((XP, channels), BF16)
    for s in range(slots):
        live = s < used
        top = slot[0, s]
        left = slot[1, s]
        base = pl.multiple_of(left // 8 * 8, 8)
        window_all = wide[pl.ds(top, side), pl.ds(base, 2 * XP), :]
        window_all = pltpu.roll(window_all, 2 * XP - (LEFT - 1) - lax.rem(left, 8), 1)
        for b in range(3):
            window = (window_all if b == 0 else pltpu.roll(window_all, 2 * XP - b, 1))[:, :XP]
            low = jnp.where(live, max(0, 1 - b), XP)
            keep = (columns >= low) & (columns < min(side, side + 1 - b))
            shifted[b, pl.ds(s * padded, XP), :] = none
            shifted[b, pl.ds(s * padded + XP, area), :] = (
                jnp.where(keep, window, 0.0).astype(BF16).reshape(area, channels)
            )
            shifted[b, pl.ds(s * padded + XP + area, XP), :] = none

    for s in range(slots):
        taps = [
            shifted[b, pl.ds(s * padded + a * XP, area), :] for a in range(3) for b in range(3)
        ]
        lhs = jnp.concatenate(taps, axis=1)
        pre = jnp.dot(lhs, weight_ref[...].reshape(9 * channels, channels), preferred_element_type=F32)
        gelu_ref[pl.ds(s * area, area), :] = gelu_slope(pre)


def list_slots(dims, own_ref, slot, fields):
    _, slots, heads, cap = dims
    width = slot.shape[0]
    for index in range(slots):
        for field in range(width):
            slot[field, index] = 0

    def head(j, used):
        count = own_ref[j]
        for r in range(cap):
            live = (r < count) & (used < slots)

            @pl.when(live)
            def _():
                for field, value in enumerate(fields(j, r)):
                    slot[field, used] = value

            used = used + live.astype(jnp.int32)
        return used

    return lax.fori_loop(0, heads, head, 0)


def slope_kernel(dims, me_ref, own_ref, ours_ref, across_ref, gelu_ref, shifted, mine_ref, theirs_ref, slope_ref,
                 slid, prior, slot):
    side, slots, heads, _ = dims
    boxes = ours_ref.shape[1]
    channels = gelu_ref.shape[1]
    area = side * XP
    padded = (side + 2) * XP
    me = me_ref[0]
    core = lax.rem(me, 2)

    lane = lax.broadcasted_iota(jnp.int32, (8, channels), 1)
    totals = jnp.zeros((8, channels), F32)
    for i in range(heads):
        row = jnp.where(core == i % 2, ours_ref[i // 2, 0, 0], across_ref[i // 2, 0, 0]).astype(F32)[8:16]
        totals = totals + jnp.where(i < me, row, 0.0)
    line = lax.broadcasted_iota(jnp.int32, (8, channels), 0)
    totals = jnp.where(line == side - 8, totals, 0.0)
    for j in range(heads):
        prior[j] = jnp.sum(jnp.where(lane == j, totals, 0.0)).astype(jnp.int32)
    used = list_slots(dims, own_ref, slot, lambda j, r: (j, jnp.minimum(prior[j] + r, boxes - 1)))

    flat_columns = lax.broadcasted_iota(jnp.int32, (side, XP, channels), 1).reshape(area, channels)
    for s in range(slots):
        chip = slot[0, s] // 2
        box = slot[1, s]
        same = lax.rem(slot[0, s], 2) == core
        upstream = jnp.where(same, ours_ref[chip, box].astype(F32), across_ref[chip, box].astype(F32))
        upstream = upstream.reshape(area, channels)
        last = jnp.where(s < used, side, 0)
        slope = upstream * gelu_ref[pl.ds(s * area, area), :]
        slope = jnp.where(flat_columns < last, slope, 0.0).astype(BF16)
        slope_ref[pl.ds(s * area, area), :] = slope
        for a in range(3):
            if a > 0:
                slid[a, pl.ds(s * padded, a * XP), :] = jnp.zeros((a * XP, channels), BF16)
            slid[a, pl.ds(s * padded + a * XP, area), :] = slope
            if a < 2:
                slid[a, pl.ds(s * padded + a * XP + area, (2 - a) * XP), :] = jnp.zeros(
                    ((2 - a) * XP, channels), BF16
                )

    half = channels // 2
    rows = channels // 8
    split = 9 * rows // 2
    for b in range(3):
        rhs = jnp.concatenate([slid[a] for a in range(3)], axis=1)
        terms = lax.dot_general(
            shifted[b], rhs, (((0,), (0,)), ((), ())), preferred_element_type=F32
        )
        for a in range(3):
            first = (3 * a + b) * rows
            for low, end, part in ((first, min(first + rows, split), 0), (max(first, split), first + rows, 1)):
                if low >= end:
                    continue
                pieces = [
                    terms[
                        (low - first) * 8 : (end - first) * 8,
                        a * channels + side_ * half : a * channels + (side_ + 1) * half,
                    ].reshape(end - low, 8, half)
                    for side_ in range(2)
                ]
                for ref, wanted in ((mine_ref, part), (theirs_ref, 1 - part)):

                    @pl.when(core == wanted)
                    def _():
                        for side_ in range(2):
                            ref[pl.ds(low - part * split, end - low), side_] = pieces[side_]


def backward_kernel(dims, own_ref, row_ref, col_ref, slope_ref, weight_ref, main_ref, spill_ref, canvas, shifted,
                    slot):
    side, slots, _, _ = dims
    high = main_ref.shape[0]
    width = main_ref.shape[1]
    channels = main_ref.shape[2]
    halo = spill_ref.shape[0]
    area = side * XP

    used = list_slots(dims, own_ref, slot, lambda j, r: (row_ref[j, r], col_ref[j, r]))
    canvas[...] = jnp.zeros(canvas.shape, F32)
    none = jnp.zeros((XP, channels), BF16)
    rhs = jnp.concatenate([weight_ref[k] for k in range(9)], axis=1)
    columns = lax.broadcasted_iota(jnp.int32, (side, XP, channels), 1)
    for s in range(slots):
        slope = slope_ref[pl.ds(s * area, area), :].astype(F32)
        for b in range(3):
            moved = slope if b == 1 else pltpu.roll(slope, (area + b - 1) % area, 0)
            shifted[b, pl.ds(0, XP), :] = none
            shifted[b, pl.ds(XP, area), :] = moved.astype(BF16)
            shifted[b, pl.ds(XP + area, XP), :] = none
        taps = [shifted[b, pl.ds((2 - a) * XP, area), :] for a in range(3) for b in range(3)]
        lhs = jnp.concatenate(taps, axis=1)
        grad = lax.dot_general(lhs, rhs, (((1,), (1,)), ((), ())), preferred_element_type=F32)
        grad = grad.astype(BF16).astype(F32).reshape(side, XP, channels)
        last = jnp.where(s < used, side, 0)
        grad = jnp.where(columns < last, grad, 0.0)
        left = slot[1, s]
        grad = jnp.concatenate([grad, jnp.zeros((side, XP // 2, channels), F32)], axis=1)
        grad = pltpu.roll(grad, lax.rem(left, 8), 1)
        base = pl.multiple_of(left // 8 * 8, 8)
        place = (pl.ds(slot[0, s], side), pl.ds(base, XP + XP // 2), slice(None))
        canvas[place] = canvas[place] + grad
    main_ref[...] = canvas[pl.ds(0, high), pl.ds(0, width), :]
    spill_ref[...] = canvas[pl.ds(high, halo), pl.ds(0, width), :].astype(spill_ref.dtype)


def finish_kernel(core_ref, mine_ref, other_ref, out_ref):
    rows = mine_ref.shape[0] // 16
    half = out_ref.shape[0] // 2
    lanes = mine_ref.shape[1]
    core = core_ref[0]
    for part in range(2):
        source = jnp.where(core == part, mine_ref[...], other_ref[...]).astype(F32)
        source = source.reshape(rows, 2, 8, lanes)
        for piece in range(2):
            out_ref[pl.ds(part * half, half), pl.ds(piece * lanes, lanes)] = source[:, piece].reshape(half, lanes)


def smem():
    return pl.BlockSpec(memory_space=pltpu.SMEM)


def vmem():
    return pl.BlockSpec(memory_space=pltpu.VMEM)


def shift(array, axis, by):
    length = lax.axis_size(axis)
    pairs = [(i, i + by) for i in range(length) if 0 <= i + by < length]
    return lax.ppermute(array, axis, pairs)


def repeated(array, times):
    return jnp.broadcast_to(array[None], (times,) + array.shape)


def on_device(feature_map, weight, mask_grad, send_count, send_row, send_col):
    tile_map = feature_map[0]
    high, width, channels = tile_map.shape
    boxes, side = mask_grad.shape[2], mask_grad.shape[3]
    heads, cap = send_row.shape[2], send_row.shape[3]
    owners = lax.axis_size("dp")
    tiles = lax.axis_size("tile")
    slots = boxes * cap
    halo = side - 1
    area, padded = side * XP, (side + 2) * XP
    dims = (side, slots, heads, cap)
    me = lax.axis_index("dp")
    me_array = me.reshape(1).astype(jnp.int32)
    own, top_rows, left_cols = send_count[0, 0], send_row[0, 0], send_col[0, 0]
    partner = [(i, i ^ 1) for i in range(owners)]
    chips = owners // 2
    same_core = [[2 * i + c for i in range(chips)] for c in range(2)]

    below = shift(tile_map[:halo], "tile", -1)
    spare = jnp.pad(own.astype(BF16), (0, channels - heads))
    spare = jnp.broadcast_to(spare, (boxes, side, XP - side, channels))
    up = jnp.concatenate([mask_grad[0, 0], spare], 2)
    sent = repeated(up, chips)
    ups = lax.all_to_all(sent, "dp", 0, 0, axis_index_groups=same_core, tiled=True)
    partner_ups = lax.ppermute(ups, "dp", partner)
    core = lax.rem(me, 2)

    gelu, shifted = pl.pallas_call(
        lambda *refs: forward_kernel(dims, *refs),
        out_shape=(
            pltpu.VMEM((slots * area, channels), F32),
            pltpu.VMEM((3, slots * padded, channels), BF16),
        ),
        in_specs=[smem()] * 3 + [vmem()] * 3,
        out_specs=(vmem(), vmem()),
        scratch_shapes=[
            pltpu.VMEM((high + halo, width + 2 * LEFT, channels), F32),
            pltpu.SMEM((2, slots), jnp.int32),
        ],
        name="forward",
        compiler_params=pltpu.CompilerParams(vmem_limit_bytes=VMEM_BYTES),
    )(own, top_rows, left_cols, tile_map, below, weight)

    lanes = channels // 2
    total = 9 * channels * 2
    split = jax.ShapeDtypeStruct((total // 32, 2, 8, lanes), F32)
    mine, theirs, slope = pl.pallas_call(
        lambda *refs: slope_kernel(dims, *refs),
        out_shape=(split, split, jax.ShapeDtypeStruct((slots * area, channels), BF16)),
        in_specs=[smem()] * 2 + [vmem()] * 4,
        out_specs=(vmem(), vmem(), vmem()),
        scratch_shapes=[
            pltpu.VMEM((3, slots * padded, channels), BF16),
            pltpu.SMEM((heads,), jnp.int32),
            pltpu.SMEM((2, slots), jnp.int32),
        ],
        name="slope",
        compiler_params=pltpu.CompilerParams(vmem_limit_bytes=VMEM_BYTES),
    )(me_array, own, ups, partner_ups, gelu, shifted)

    main, spill = pl.pallas_call(
        lambda *refs: backward_kernel(dims, *refs),
        out_shape=(
            jax.ShapeDtypeStruct((high, width, channels), F32),
            jax.ShapeDtypeStruct((halo, width, channels), BF16),
        ),
        in_specs=[smem()] * 3 + [vmem()] * 2,
        out_specs=(vmem(), vmem()),
        scratch_shapes=[
            pltpu.VMEM((high + halo, width + XP, channels), F32),
            pltpu.VMEM((3, padded, channels), BF16),
            pltpu.SMEM((2, slots), jnp.int32),
        ],
        name="backward",
        compiler_params=pltpu.CompilerParams(vmem_limit_bytes=VMEM_BYTES),
    )(own, top_rows, left_cols, slope, weight)
    arriving = shift(spill, "tile", 1).astype(F32)
    map_grad = jnp.concatenate([main[:halo] + arriving, main[halo:]], 0)

    part = total // 2
    deep = 16 if tiles % 16 == 0 else 1
    wide = tiles // deep
    plane = [
        [(x * deep + z) * owners + 2 * y + c for x in range(wide) for y in range(chips)]
        for z in range(deep)
        for c in range(2)
    ]
    stick = [[x * deep + z for z in range(deep)] for x in range(wide)]
    near = wide * chips
    pair = (mine.reshape(part, lanes) + lax.ppermute(theirs, "dp", partner).reshape(part, lanes)).astype(BF16)
    got = lax.all_to_all(
        pair.reshape(near, part // near, lanes), ("tile", "dp"), 0, 0, axis_index_groups=plane, tiled=True
    )
    column = got.astype(F32).sum(0)
    got = lax.all_to_all(
        column.reshape(deep, part // near // deep, lanes), "tile", 0, 0, axis_index_groups=stick, tiled=True
    )
    chunk = (got.sum(0) / (boxes * tiles * owners)).astype(BF16)
    got = lax.all_to_all(repeated(chunk, deep), "tile", 0, 0, axis_index_groups=stick, tiled=True)
    got = got.reshape(part // near, lanes)
    got = lax.all_to_all(repeated(got, near), ("tile", "dp"), 0, 0, axis_index_groups=plane, tiled=True)
    got = got.reshape(part, lanes)
    other = lax.ppermute(got, "dp", partner)
    weight_grad = pl.pallas_call(
        finish_kernel,
        out_shape=jax.ShapeDtypeStruct((9 * channels, channels), F32),
        in_specs=[smem(), vmem(), vmem()],
        out_specs=vmem(),
        name="finish",
        compiler_params=pltpu.CompilerParams(vmem_limit_bytes=VMEM_BYTES),
    )(core.reshape(1), got, other)
    return map_grad[None], weight_grad.reshape(9, channels, channels)


def solution(mesh):
    in_specs = (
        P("dp", "tile", None, None),
        P(),
        P("dp", "tile", None, None, None, None),
        P("dp", "tile", None),
        P("dp", "tile", None, None),
        P("dp", "tile", None, None),
    )
    out_specs = (P("dp", "tile", None, None), P())

    return jax.shard_map(on_device, mesh=mesh, in_specs=in_specs, out_specs=out_specs, check_vma=False)
```

```python
import jax
import jax.numpy as jnp
from jax import lax
from jax.experimental import pallas as pl
from jax.experimental.pallas import tpu as pltpu
from jax.sharding import PartitionSpec as P


GELU_SCALE = 0.7978845608
GELU_CUBIC = 0.044715
F32 = jnp.float32
BF16 = jnp.bfloat16
VMEM_BYTES = 20 * 2**20
XP = 16
LEFT = 8


def gelu_slope(values):
    inner = GELU_SCALE * (values + GELU_CUBIC * values * values * values)
    tangent = jnp.tanh(inner)
    outer = (
        0.5
        * values
        * (1.0 - tangent * tangent)
        * GELU_SCALE
        * (1.0 + 3.0 * GELU_CUBIC * values * values)
    )
    return 0.5 * (1.0 + tangent) + outer


def list_slots(dims, count_of, slot, fields):
    _, slots, heads, cap = dims
    width = slot.shape[0]
    for index in range(slots):
        for field in range(width):
            slot[field, index] = 0

    def head(j, used):
        count = count_of(j)
        for r in range(cap):
            live = (r < count) & (used < slots)

            @pl.when(live)
            def _():
                for field, value in enumerate(fields(j, r)):
                    slot[field, used] = value

            used = used + live.astype(jnp.int32)
        return used

    return lax.fori_loop(0, heads, head, 0)


def crop_kernel(dims, own_ref, row_ref, col_ref, map_ref, below_ref, crop_ref, wide, slot):
    side, slots, _, _ = dims
    high, width, channels = map_ref.shape
    halo = side - 1
    area = side * XP
    used = list_slots(dims, lambda j: own_ref[j], slot, lambda j, r: (row_ref[j, r], col_ref[j, r]))

    wide[pl.ds(0, high), pl.ds(LEFT, width), :] = map_ref[...].astype(F32)
    wide[pl.ds(high, halo), pl.ds(LEFT, width), :] = below_ref[pl.ds(0, halo)].astype(F32)

    columns = lax.broadcasted_iota(jnp.int32, (side, XP, channels), 1)
    for s in range(slots):
        left = slot[1, s]
        base = pl.multiple_of(left // 8 * 8, 8)
        window = wide[pl.ds(slot[0, s], side), pl.ds(base + LEFT, 3 * XP // 2), :]
        window = pltpu.roll(window, lax.rem(3 * XP // 2 - lax.rem(left, 8), 3 * XP // 2), 1)[:, :XP]
        last = jnp.where(s < used, side, 0)
        window = jnp.where(columns < last, window, 0.0).astype(BF16)
        crop_ref[pl.ds(s * area, area), :] = window.reshape(area, channels)


def forward_kernel(dims, me_ref, own_ref, other_ref, weight_ref, gelu_ref, gelu_other_ref, shifted):
    side, slots, _, _ = dims
    channels = own_ref.shape[1]
    half = channels // 2
    area = side * XP
    padded = (side + 2) * XP
    core = lax.rem(me_ref[0], 2)
    lanes = pl.ds(pl.multiple_of(core * half, half), half)

    none = jnp.zeros((XP, channels), BF16)
    for s in range(2 * slots):
        source = own_ref if s < slots else other_ref
        crop = source[pl.ds(s % slots * area, area), :]
        loose = crop.astype(F32)
        for b in range(3):
            moved = crop if b == 1 else pltpu.roll(loose, (area + 1 - b) % area, 0).astype(BF16)
            shifted[b, pl.ds(s * padded, XP), :] = none
            shifted[b, pl.ds(s * padded + XP, area), :] = moved
            shifted[b, pl.ds(s * padded + XP + area, XP), :] = none

    for s in range(2 * slots):
        taps = [
            shifted[b, pl.ds(s * padded + a * XP, area), :] for a in range(3) for b in range(3)
        ]
        lhs = jnp.concatenate(taps, axis=1)
        rows = pl.ds(s % slots * area, area)
        if s < slots:
            matrix = weight_ref[...].reshape(9 * channels, channels)
            gelu_ref[rows, :] = gelu_slope(jnp.dot(lhs, matrix, preferred_element_type=F32))
        else:
            matrix = weight_ref[:, :, lanes].reshape(9 * channels, half)
            gelu_other_ref[rows, :] = gelu_slope(jnp.dot(lhs, matrix, preferred_element_type=F32))


def slope_kernel(dims, me_ref, own_ref, ours_ref, across_ref, gelu_ref, gelu_other_ref, shifted,
                 terms_ref, slope_ref, slid, prior, partner_count, slot, partner_slot):
    side, slots, heads, _ = dims
    boxes = ours_ref.shape[1]
    channels = gelu_ref.shape[1]
    half = channels // 2
    area = side * XP
    padded = (side + 2) * XP
    me = me_ref[0]
    core = lax.rem(me, 2)
    even = me - core
    partner = even + 1 - core
    lanes = pl.ds(pl.multiple_of(core * half, half), half)

    lane = lax.broadcasted_iota(jnp.int32, (8, channels), 1)
    line = lax.broadcasted_iota(jnp.int32, (8, channels), 0)
    totals = jnp.zeros((8, channels), F32)
    counts = jnp.zeros((8, channels), F32)
    for i in range(heads):
        row = jnp.where(core == i % 2, ours_ref[i // 2, 0, 0], across_ref[i // 2, 0, 0]).astype(F32)[8:16]
        totals = totals + jnp.where(i < even, row, 0.0)
        counts = counts + jnp.where(i == partner, row, 0.0)
    totals = jnp.where(line == side - 8, totals, 0.0)
    counts = jnp.where(line == side - 8, counts, 0.0)
    for j in range(heads):
        prior[j] = jnp.sum(jnp.where(lane == j, totals, 0.0)).astype(jnp.int32)
        partner_count[j] = jnp.sum(jnp.where(lane == j, counts, 0.0)).astype(jnp.int32)

    def box(j, r, ahead):
        return j, jnp.minimum(prior[j] + ahead + r, boxes - 1)

    used = list_slots(
        dims, lambda j: own_ref[j], slot, lambda j, r: box(j, r, core * partner_count[j])
    )
    partner_used = list_slots(
        dims, lambda j: partner_count[j], partner_slot, lambda j, r: box(j, r, (1 - core) * own_ref[j])
    )

    def masked(slope, last, width):
        columns = lax.broadcasted_iota(jnp.int32, (side, XP, width), 1).reshape(area, width)
        return jnp.where(columns < last, slope, 0.0).astype(BF16)

    for s in range(2 * slots):
        table, number, count = (slot, s, used) if s < slots else (partner_slot, s - slots, partner_used)
        chip = table[0, number] // 2
        index = table[1, number]
        same = lax.rem(table[0, number], 2) == core
        last = jnp.where(number < count, side, 0)
        rows = pl.ds(number * area, area)
        if s < slots:
            upstream = jnp.where(same, ours_ref[chip, index], across_ref[chip, index]).astype(F32)
            slope = masked(upstream.reshape(area, channels) * gelu_ref[rows, :], last, channels)
            slope_ref[rows, :] = slope
            slope = jnp.where(core == 0, slope[:, :half], slope[:, half:])
        else:
            upstream = jnp.where(
                same, ours_ref[chip, index, :, :, lanes], across_ref[chip, index, :, :, lanes]
            ).astype(F32)
            slope = masked(upstream.reshape(area, half) * gelu_other_ref[rows, :], last, half)
        for a in range(3):
            if a > 0:
                slid[a, pl.ds(s * padded, a * XP), :] = jnp.zeros((a * XP, half), BF16)
            slid[a, pl.ds(s * padded + a * XP, area), :] = slope
            if a < 2:
                slid[a, pl.ds(s * padded + a * XP + area, (2 - a) * XP), :] = jnp.zeros(
                    ((2 - a) * XP, half), BF16
                )

    rhs = jnp.concatenate([slid[a] for a in range(3)], axis=1)
    for b in range(3):
        terms = lax.dot_general(
            shifted[b], rhs, (((0,), (0,)), ((), ())), preferred_element_type=F32
        )
        for a in range(3):
            terms_ref[pl.ds((3 * a + b) * channels, channels), :] = (
                terms[:, a * half : (a + 1) * half].astype(BF16)
            )


def backward_kernel(dims, own_ref, row_ref, col_ref, slope_ref, weight_ref, main_ref, spill_ref, canvas, shifted,
                    slot):
    side, slots, _, _ = dims
    high = main_ref.shape[0]
    width = main_ref.shape[1]
    channels = main_ref.shape[2]
    halo = spill_ref.shape[0]
    area = side * XP

    used = list_slots(dims, lambda j: own_ref[j], slot, lambda j, r: (row_ref[j, r], col_ref[j, r]))
    canvas[...] = jnp.zeros(canvas.shape, F32)
    none = jnp.zeros((XP, channels), BF16)
    rhs = jnp.concatenate([weight_ref[k] for k in range(9)], axis=1)
    columns = lax.broadcasted_iota(jnp.int32, (side, XP, channels), 1)
    for s in range(slots):
        slope = slope_ref[pl.ds(s * area, area), :].astype(F32)
        for b in range(3):
            moved = slope if b == 1 else pltpu.roll(slope, (area + b - 1) % area, 0)
            shifted[b, pl.ds(0, XP), :] = none
            shifted[b, pl.ds(XP, area), :] = moved.astype(BF16)
            shifted[b, pl.ds(XP + area, XP), :] = none
        taps = [shifted[b, pl.ds((2 - a) * XP, area), :] for a in range(3) for b in range(3)]
        lhs = jnp.concatenate(taps, axis=1)
        grad = lax.dot_general(lhs, rhs, (((1,), (1,)), ((), ())), preferred_element_type=F32)
        grad = grad.astype(BF16).astype(F32).reshape(side, XP, channels)
        last = jnp.where(s < used, side, 0)
        grad = jnp.where(columns < last, grad, 0.0)
        left = slot[1, s]
        grad = jnp.concatenate([grad, jnp.zeros((side, XP // 2, channels), F32)], axis=1)
        grad = pltpu.roll(grad, lax.rem(left, 8), 1)
        base = pl.multiple_of(left // 8 * 8, 8)
        place = (pl.ds(slot[0, s], side), pl.ds(base, XP + XP // 2), slice(None))
        canvas[place] = canvas[place] + grad
    main_ref[...] = canvas[pl.ds(0, high), pl.ds(0, width), :]
    spill_ref[...] = canvas[pl.ds(high, halo), pl.ds(0, width), :].astype(spill_ref.dtype)


def finish_kernel(core_ref, mine_ref, other_ref, out_ref):
    half = mine_ref.shape[1]
    core = core_ref[0]
    for part in range(2):
        source = jnp.where(core == part, mine_ref[...], other_ref[...])
        out_ref[:, pl.ds(part * half, half)] = source.astype(F32)


def smem():
    return pl.BlockSpec(memory_space=pltpu.SMEM)


def vmem():
    return pl.BlockSpec(memory_space=pltpu.VMEM)


def kernel(body, dims, out_shape, in_specs, scratch_shapes):
    return pl.pallas_call(
        lambda *refs: body(dims, *refs),
        out_shape=out_shape,
        in_specs=in_specs,
        out_specs=jax.tree.map(lambda _: vmem(), out_shape),
        scratch_shapes=scratch_shapes,
        compiler_params=pltpu.CompilerParams(vmem_limit_bytes=VMEM_BYTES),
    )


def shift(array, axis, by):
    length = lax.axis_size(axis)
    pairs = [(i, i + by) for i in range(length) if 0 <= i + by < length]
    return lax.ppermute(array, axis, pairs)


def repeated(array, times):
    return jnp.broadcast_to(array[None], (times,) + array.shape)


def on_device(feature_map, weight, mask_grad, send_count, send_row, send_col):
    tile_map = feature_map[0]
    high, width, channels = tile_map.shape
    boxes, side = mask_grad.shape[2], mask_grad.shape[3]
    heads, cap = send_row.shape[2], send_row.shape[3]
    owners = lax.axis_size("dp")
    tiles = lax.axis_size("tile")
    slots = boxes * cap
    halo = side - 1
    area, padded = side * XP, (side + 2) * XP
    dims = (side, slots, heads, cap)
    me = lax.axis_index("dp")
    me_array = me.reshape(1).astype(jnp.int32)
    own, top_rows, left_cols = send_count[0, 0], send_row[0, 0], send_col[0, 0]
    partner = [(i, i ^ 1) for i in range(owners)]
    chips = owners // 2
    same_core = [[2 * i + c for i in range(chips)] for c in range(2)]

    half = channels // 2
    core = lax.rem(me, 2)

    below = shift(tile_map, "tile", -1)
    spare = jnp.pad(own.astype(BF16), (0, channels - heads))
    spare = jnp.broadcast_to(spare, (boxes, side, XP - side, channels))
    up = jnp.concatenate([mask_grad[0, 0], spare], 2)
    sent = repeated(up, chips)
    ups = lax.all_to_all(sent, "dp", 0, 0, axis_index_groups=same_core, tiled=True)
    partner_ups = lax.ppermute(ups, "dp", partner)

    crops = kernel(
        crop_kernel,
        dims,
        jax.ShapeDtypeStruct((slots * area, channels), BF16),
        [smem()] * 3 + [vmem()] * 2,
        [
            pltpu.VMEM((high + halo, width + 2 * LEFT, channels), F32),
            pltpu.SMEM((2, slots), jnp.int32),
        ],
    )(own, top_rows, left_cols, tile_map, below)
    partner_crops = lax.ppermute(crops, "dp", partner)

    gelu, gelu_other, shifted = kernel(
        forward_kernel,
        dims,
        (
            pltpu.VMEM((slots * area, channels), F32),
            pltpu.VMEM((slots * area, half), F32),
            pltpu.VMEM((3, 2 * slots * padded, channels), BF16),
        ),
        [smem()] + [vmem()] * 3,
        [],
    )(me_array, crops, partner_crops, weight)

    terms, slope = kernel(
        slope_kernel,
        dims,
        (
            jax.ShapeDtypeStruct((9 * channels, half), BF16),
            jax.ShapeDtypeStruct((slots * area, channels), BF16),
        ),
        [smem()] * 2 + [vmem()] * 5,
        [
            pltpu.VMEM((3, 2 * slots * padded, half), BF16),
            pltpu.SMEM((heads,), jnp.int32),
            pltpu.SMEM((heads,), jnp.int32),
            pltpu.SMEM((2, slots), jnp.int32),
            pltpu.SMEM((2, slots), jnp.int32),
        ],
    )(me_array, own, ups, partner_ups, gelu, gelu_other, shifted)

    main, spill = pl.pallas_call(
        lambda *refs: backward_kernel(dims, *refs),
        out_shape=(
            jax.ShapeDtypeStruct((high, width, channels), F32),
            jax.ShapeDtypeStruct((halo, width, channels), BF16),
        ),
        in_specs=[smem()] * 3 + [vmem()] * 2,
        out_specs=(vmem(), vmem()),
        scratch_shapes=[
            pltpu.VMEM((high + halo, width + XP, channels), F32),
            pltpu.VMEM((3, padded, channels), BF16),
            pltpu.SMEM((2, slots), jnp.int32),
        ],
        name="backward",
        compiler_params=pltpu.CompilerParams(vmem_limit_bytes=VMEM_BYTES),
    )(own, top_rows, left_cols, slope, weight)
    arriving = shift(spill, "tile", 1)
    arriving = arriving.astype(F32)
    map_grad = jnp.concatenate([main[:halo] + arriving, main[halo:]], 0)

    part = 9 * channels
    deep = 16 if tiles % 16 == 0 else 1
    wide = tiles // deep
    plane = [
        [(x * deep + z) * owners + 2 * y + c for x in range(wide) for y in range(chips)]
        for z in range(deep)
        for c in range(2)
    ]
    stick = [[x * deep + z for z in range(deep)] for x in range(wide)]
    near = wide * chips
    got = lax.all_to_all(
        terms.reshape(near, part // near, half), ("tile", "dp"), 0, 0, axis_index_groups=plane, tiled=True
    )
    column = got.astype(F32).sum(0)
    got = lax.all_to_all(
        column.reshape(deep, part // near // deep, half), "tile", 0, 0, axis_index_groups=stick, tiled=True
    )
    chunk = (got.sum(0) / (boxes * tiles * owners)).astype(BF16)
    got = lax.all_to_all(repeated(chunk, deep), "tile", 0, 0, axis_index_groups=stick, tiled=True)
    got = got.reshape(part // near, half)
    got = lax.all_to_all(repeated(got, near), ("tile", "dp"), 0, 0, axis_index_groups=plane, tiled=True)
    got = got.reshape(part, half)
    other = lax.ppermute(got, "dp", partner)
    weight_grad = pl.pallas_call(
        finish_kernel,
        out_shape=jax.ShapeDtypeStruct((9 * channels, channels), F32),
        in_specs=[smem(), vmem(), vmem()],
        out_specs=vmem(),
        name="finish",
        compiler_params=pltpu.CompilerParams(vmem_limit_bytes=VMEM_BYTES),
    )(core.reshape(1), got, other)
    return map_grad[None], weight_grad.reshape(9, channels, channels)


def solution(mesh):
    in_specs = (
        P("dp", "tile", None, None),
        P(),
        P("dp", "tile", None, None, None, None),
        P("dp", "tile", None),
        P("dp", "tile", None, None),
        P("dp", "tile", None, None),
    )
    out_specs = (P("dp", "tile", None, None), P())

    return jax.shard_map(
        on_device, mesh=mesh, in_specs=in_specs, out_specs=out_specs, check_vma=False
    )
```

```python
import jax
import jax.numpy as jnp
from jax import lax
from jax.experimental import pallas as pl
from jax.experimental.pallas import tpu as pltpu
from jax.sharding import PartitionSpec as P


GELU_SCALE = 0.7978845608
GELU_CUBIC = 0.044715
F32 = jnp.float32
BF16 = jnp.bfloat16
VMEM_BYTES = 20 * 2**20
XP = 16
LEFT = 8


def gelu_slope(values):
    inner = GELU_SCALE * (values + GELU_CUBIC * values * values * values)
    tangent = jnp.tanh(inner)
    outer = (
        0.5
        * values
        * (1.0 - tangent * tangent)
        * GELU_SCALE
        * (1.0 + 3.0 * GELU_CUBIC * values * values)
    )
    return 0.5 * (1.0 + tangent) + outer


def list_slots(dims, count_of, slot, fields):
    _, slots, heads, cap = dims
    width = slot.shape[0]
    for index in range(slots):
        for field in range(width):
            slot[field, index] = 0

    def head(j, used):
        count = count_of(j)
        for r in range(cap):
            live = (r < count) & (used < slots)

            @pl.when(live)
            def _():
                for field, value in enumerate(fields(j, r)):
                    slot[field, used] = value

            used = used + live.astype(jnp.int32)
        return used

    return lax.fori_loop(0, heads, head, 0)


def crop_kernel(dims, own_ref, row_ref, col_ref, map_ref, below_ref, crop_ref, wide, slot):
    side, slots, _, _ = dims
    high, width, channels = map_ref.shape
    halo = side - 1
    area = side * XP
    used = list_slots(dims, lambda j: own_ref[j], slot, lambda j, r: (row_ref[j, r], col_ref[j, r]))

    wide[pl.ds(0, high), pl.ds(LEFT, width), :] = map_ref[...].astype(F32)
    wide[pl.ds(high, halo), pl.ds(LEFT, width), :] = below_ref[pl.ds(0, halo)].astype(F32)

    columns = lax.broadcasted_iota(jnp.int32, (side, XP, channels), 1)
    for s in range(slots):
        left = slot[1, s]
        base = pl.multiple_of(left // 8 * 8, 8)
        window = wide[pl.ds(slot[0, s], side), pl.ds(base + LEFT, 3 * XP // 2), :]
        window = pltpu.roll(window, lax.rem(3 * XP // 2 - lax.rem(left, 8), 3 * XP // 2), 1)[:, :XP]
        last = jnp.where(s < used, side, 0)
        window = jnp.where(columns < last, window, 0.0).astype(BF16)
        crop_ref[pl.ds(s * area, area), :] = window.reshape(area, channels)


def forward_kernel(dims, me_ref, own_ref, other_ref, weight_ref, gelu_ref, shifted):
    side, slots, _, _ = dims
    channels = own_ref.shape[1]
    half = channels // 2
    area = side * XP
    padded = (side + 2) * XP
    core = lax.rem(me_ref[0], 2)
    lanes = pl.ds(pl.multiple_of(core * half, half), half)

    none = jnp.zeros((XP, channels), BF16)
    for s in range(2 * slots):
        source = own_ref if s < slots else other_ref
        crop = source[pl.ds(s % slots * area, area), :]
        loose = crop.astype(F32)
        for b in range(3):
            moved = crop if b == 1 else pltpu.roll(loose, (area + 1 - b) % area, 0).astype(BF16)
            shifted[b, pl.ds(s * padded, XP), :] = none
            shifted[b, pl.ds(s * padded + XP, area), :] = moved
            shifted[b, pl.ds(s * padded + XP + area, XP), :] = none

    matrix = weight_ref[:, :, lanes].reshape(9 * channels, half)
    for s in range(2 * slots):
        taps = [
            shifted[b, pl.ds(s * padded + a * XP, area), :] for a in range(3) for b in range(3)
        ]
        lhs = jnp.concatenate(taps, axis=1)
        gelu_ref[pl.ds(s * area, area), :] = gelu_slope(
            jnp.dot(lhs, matrix, preferred_element_type=F32)
        )


def slope_kernel(dims, me_ref, own_ref, ours_ref, across_ref, gelu_ref, shifted,
                 terms_ref, slope_ref, lent_ref, slid, prior, partner_count, slot, partner_slot, staged, sems):
    side, slots, heads, _ = dims
    boxes = ours_ref.shape[1]
    half = gelu_ref.shape[1]
    channels = 2 * half
    area = side * XP
    padded = (side + 2) * XP
    me = me_ref[0]
    core = lax.rem(me, 2)
    even = me - core
    partner = even + 1 - core
    lanes = pl.ds(pl.multiple_of(core * half, half), half)

    lane = lax.broadcasted_iota(jnp.int32, (8, half), 1)
    line = lax.broadcasted_iota(jnp.int32, (8, half), 0)
    totals = jnp.zeros((8, half), F32)
    counts = jnp.zeros((8, half), F32)
    for i in range(heads):
        row = jnp.where(
            core == i % 2, ours_ref[i // 2, 0, 0, :, :half], across_ref[i // 2, 0, 0, :, :half]
        ).astype(F32)[8:16]
        totals = totals + jnp.where(i < even, row, 0.0)
        counts = counts + jnp.where(i == partner, row, 0.0)
    totals = jnp.where(line == side - 8, totals, 0.0)
    counts = jnp.where(line == side - 8, counts, 0.0)
    for j in range(heads):
        prior[j] = jnp.sum(jnp.where(lane == j, totals, 0.0)).astype(jnp.int32)
        partner_count[j] = jnp.sum(jnp.where(lane == j, counts, 0.0)).astype(jnp.int32)

    def box(j, r, ahead):
        return j, jnp.minimum(prior[j] + ahead + r, boxes - 1)

    used = list_slots(
        dims, lambda j: own_ref[j], slot, lambda j, r: box(j, r, core * partner_count[j])
    )
    partner_used = list_slots(
        dims, lambda j: partner_count[j], partner_slot, lambda j, r: box(j, r, (1 - core) * own_ref[j])
    )

    columns = lax.broadcasted_iota(jnp.int32, (side, XP, half), 1).reshape(area, half)
    for s in range(2 * slots):
        table, number, count, ref = (
            (slot, s, used, slope_ref) if s < slots else (partner_slot, s - slots, partner_used, lent_ref)
        )
        head = table[0, number]
        where = (head // 2, table[1, number], slice(None), slice(None), lanes)
        upstream = jnp.where(lax.rem(head, 2) == core, ours_ref[where], across_ref[where]).astype(F32)
        last = jnp.where(number < count, side, 0)
        slope = upstream.reshape(area, half) * gelu_ref[pl.ds(s * area, area), :]
        slope = jnp.where(columns < last, slope, 0.0).astype(BF16)
        ref[pl.ds(number * area, area), :] = slope
        for a in range(3):
            if a > 0:
                slid[a, pl.ds(s * padded, a * XP), :] = jnp.zeros((a * XP, half), BF16)
            slid[a, pl.ds(s * padded + a * XP, area), :] = slope
            if a < 2:
                slid[a, pl.ds(s * padded + a * XP + area, (2 - a) * XP), :] = jnp.zeros(
                    ((2 - a) * XP, half), BF16
                )

    rhs = jnp.concatenate([slid[a] for a in range(3)], axis=1)
    copies = []
    for b in range(3):
        terms = lax.dot_general(
            shifted[b], rhs, (((0,), (0,)), ((), ())), preferred_element_type=F32
        )
        for a in range(3):
            tap = 3 * a + b
            rows = pl.ds(tap * channels, channels)
            staged[rows, :] = terms[:, a * half : (a + 1) * half].astype(BF16)
            copy = pltpu.make_async_copy(staged.at[rows], terms_ref.at[rows], sems.at[tap])
            copy.start()
            copies.append(copy)
    for copy in copies:
        copy.wait()


def backward_kernel(dims, me_ref, own_ref, row_ref, col_ref, slope_ref, back_ref, weight_ref, main_ref, spill_ref, canvas, shifted,
                    slot):
    side, slots, _, _ = dims
    high = main_ref.shape[0]
    width = main_ref.shape[1]
    channels = main_ref.shape[2]
    halo = spill_ref.shape[0]
    area = side * XP

    used = list_slots(dims, lambda j: own_ref[j], slot, lambda j, r: (row_ref[j, r], col_ref[j, r]))
    core = lax.rem(me_ref[0], 2)
    canvas[...] = jnp.zeros(canvas.shape, F32)
    none = jnp.zeros((XP, channels), BF16)
    rhs = jnp.concatenate([weight_ref[k] for k in range(9)], axis=1)
    columns = lax.broadcasted_iota(jnp.int32, (side, XP, channels), 1)
    for s in range(slots):
        ours = slope_ref[pl.ds(s * area, area), :].astype(F32)
        theirs = back_ref[pl.ds(s * area, area), :].astype(F32)
        slope = jnp.concatenate(
            [jnp.where(core == 0, ours, theirs), jnp.where(core == 0, theirs, ours)], axis=1
        )
        for b in range(3):
            moved = slope if b == 1 else pltpu.roll(slope, (area + b - 1) % area, 0)
            shifted[b, pl.ds(0, XP), :] = none
            shifted[b, pl.ds(XP, area), :] = moved.astype(BF16)
            shifted[b, pl.ds(XP + area, XP), :] = none
        taps = [shifted[b, pl.ds((2 - a) * XP, area), :] for a in range(3) for b in range(3)]
        lhs = jnp.concatenate(taps, axis=1)
        grad = lax.dot_general(lhs, rhs, (((1,), (1,)), ((), ())), preferred_element_type=F32)
        grad = grad.astype(BF16).astype(F32).reshape(side, XP, channels)
        last = jnp.where(s < used, side, 0)
        grad = jnp.where(columns < last, grad, 0.0)
        left = slot[1, s]
        grad = jnp.concatenate([grad, jnp.zeros((side, XP // 2, channels), F32)], axis=1)
        grad = pltpu.roll(grad, lax.rem(left, 8), 1)
        base = pl.multiple_of(left // 8 * 8, 8)
        place = (pl.ds(slot[0, s], side), pl.ds(base, XP + XP // 2), slice(None))
        canvas[place] = canvas[place] + grad
    main_ref[...] = canvas[pl.ds(0, high), pl.ds(0, width), :]
    spill_ref[...] = canvas[pl.ds(high, halo), pl.ds(0, width), :].astype(spill_ref.dtype)


def finish_kernel(core_ref, mine_ref, other_ref, out_ref):
    half = mine_ref.shape[1]
    core = core_ref[0]
    for part in range(2):
        source = jnp.where(core == part, mine_ref[...], other_ref[...])
        out_ref[:, pl.ds(part * half, half)] = source.astype(F32)


def smem():
    return pl.BlockSpec(memory_space=pltpu.SMEM)


def vmem():
    return pl.BlockSpec(memory_space=pltpu.VMEM)


def kernel(body, dims, out_shape, in_specs, scratch_shapes, out_specs=None):
    return pl.pallas_call(
        lambda *refs: body(dims, *refs),
        out_shape=out_shape,
        in_specs=in_specs,
        out_specs=out_specs or jax.tree.map(lambda _: vmem(), out_shape),
        scratch_shapes=scratch_shapes,
        compiler_params=pltpu.CompilerParams(vmem_limit_bytes=VMEM_BYTES),
    )


def shift(array, axis, by):
    length = lax.axis_size(axis)
    pairs = [(i, i + by) for i in range(length) if 0 <= i + by < length]
    return lax.ppermute(array, axis, pairs)


def repeated(array, times):
    return jnp.broadcast_to(array[None], (times,) + array.shape)


def on_device(feature_map, weight, mask_grad, send_count, send_row, send_col):
    tile_map = feature_map[0]
    high, width, channels = tile_map.shape
    boxes, side = mask_grad.shape[2], mask_grad.shape[3]
    heads, cap = send_row.shape[2], send_row.shape[3]
    owners = lax.axis_size("dp")
    tiles = lax.axis_size("tile")
    slots = boxes * cap
    halo = side - 1
    area, padded = side * XP, (side + 2) * XP
    dims = (side, slots, heads, cap)
    me = lax.axis_index("dp")
    me_array = me.reshape(1).astype(jnp.int32)
    own, top_rows, left_cols = send_count[0, 0], send_row[0, 0], send_col[0, 0]
    partner = [(i, i ^ 1) for i in range(owners)]
    chips = owners // 2
    same_core = [[2 * i + c for i in range(chips)] for c in range(2)]

    half = channels // 2
    core = lax.rem(me, 2)

    below = shift(tile_map[:halo], "tile", -1)
    spare = jnp.pad(own.astype(BF16), (0, channels - heads))
    spare = jnp.broadcast_to(spare, (boxes, side, XP - side, channels))
    sent = repeated(jnp.concatenate([mask_grad[0, 0], spare], 2), chips)
    ups = lax.all_to_all(sent, "dp", 0, 0, axis_index_groups=same_core, tiled=True)
    partner_ups = lax.ppermute(ups, "dp", partner)

    crops = kernel(
        crop_kernel,
        dims,
        jax.ShapeDtypeStruct((slots * area, channels), BF16),
        [smem()] * 3 + [vmem()] * 2,
        [
            pltpu.VMEM((high + halo, width + 2 * LEFT, channels), F32),
            pltpu.SMEM((2, slots), jnp.int32),
        ],
    )(own, top_rows, left_cols, tile_map, below)
    partner_crops = lax.ppermute(crops, "dp", partner)

    gelu, shifted = kernel(
        forward_kernel,
        dims,
        (
            pltpu.VMEM((2 * slots * area, half), F32),
            pltpu.VMEM((3, 2 * slots * padded, channels), BF16),
        ),
        [smem()] + [vmem()] * 3,
        [],
    )(me_array, crops, partner_crops, weight)

    strip = jax.ShapeDtypeStruct((slots * area, half), BF16)
    terms, slope, lent = kernel(
        slope_kernel,
        dims,
        (jax.ShapeDtypeStruct((9 * channels, half), BF16), strip, strip),
        [smem()] * 2 + [vmem()] * 4,
        [
            pltpu.VMEM((3, 2 * slots * padded, half), BF16),
            pltpu.SMEM((heads,), jnp.int32),
            pltpu.SMEM((heads,), jnp.int32),
            pltpu.SMEM((2, slots), jnp.int32),
            pltpu.SMEM((2, slots), jnp.int32),
            pltpu.VMEM((9 * channels, half), BF16),
            pltpu.SemaphoreType.DMA((9,)),
        ],
        out_specs=(pl.BlockSpec(memory_space=pltpu.HBM), vmem(), vmem()),
    )(me_array, own, ups, partner_ups, gelu, shifted)
    returned = lax.ppermute(lent, "dp", partner)

    main, spill = kernel(
        backward_kernel,
        dims,
        (
            jax.ShapeDtypeStruct((high, width, channels), F32),
            jax.ShapeDtypeStruct((halo, width, channels), BF16),
        ),
        [smem()] * 4 + [vmem()] * 3,
        [
            pltpu.VMEM((high + halo, width + XP, channels), F32),
            pltpu.VMEM((3, padded, channels), BF16),
            pltpu.SMEM((2, slots), jnp.int32),
        ],
    )(me_array, own, top_rows, left_cols, slope, returned, weight)
    arriving = shift(spill, "tile", 1)
    map_grad = jnp.concatenate([main[:halo] + arriving.astype(F32), main[halo:]], 0)

    part = 9 * channels
    deep = 16 if tiles % 16 == 0 else 1
    wide = tiles // deep
    plane = [
        [(x * deep + z) * owners + 2 * y + c for x in range(wide) for y in range(chips)]
        for z in range(deep)
        for c in range(2)
    ]
    stick = [[x * deep + z for z in range(deep)] for x in range(wide)]
    near = wide * chips
    got = lax.all_to_all(
        terms.reshape(near, part // near, half), ("tile", "dp"), 0, 0, axis_index_groups=plane, tiled=True
    )
    column = (got.astype(F32).sum(0) / boxes).astype(BF16)
    got = lax.all_to_all(
        column.reshape(deep, part // near // deep, half), "tile", 0, 0, axis_index_groups=stick, tiled=True
    )
    chunk = (got.astype(F32).sum(0) / (tiles * owners)).astype(BF16)
    got = lax.all_to_all(repeated(chunk, deep), "tile", 0, 0, axis_index_groups=stick, tiled=True)
    got = got.reshape(part // near, half)
    got = lax.all_to_all(
        repeated(got, near), ("tile", "dp"), 0, 0, axis_index_groups=plane, tiled=True
    )
    got = got.reshape(part, half)
    other = lax.ppermute(got, "dp", partner)
    weight_grad = pl.pallas_call(
        finish_kernel,
        out_shape=jax.ShapeDtypeStruct((9 * channels, channels), F32),
        in_specs=[smem(), vmem(), vmem()],
        out_specs=vmem(),
        name="finish",
        compiler_params=pltpu.CompilerParams(vmem_limit_bytes=VMEM_BYTES),
    )(core.reshape(1), got, other)
    return map_grad[None], weight_grad.reshape(9, channels, channels)


def solution(mesh):
    in_specs = (
        P("dp", "tile", None, None),
        P(),
        P("dp", "tile", None, None, None, None),
        P("dp", "tile", None),
        P("dp", "tile", None, None),
        P("dp", "tile", None, None),
    )
    out_specs = (P("dp", "tile", None, None), P())

    return jax.shard_map(
        on_device, mesh=mesh, in_specs=in_specs, out_specs=out_specs, check_vma=False
    )
```

```python
import jax
import jax.numpy as jnp
from jax import lax
from jax.experimental import pallas as pl
from jax.experimental.pallas import tpu as pltpu
from jax.sharding import PartitionSpec as P


GELU_SCALE = 0.7978845608
GELU_CUBIC = 0.044715
F32 = jnp.float32
BF16 = jnp.bfloat16
VMEM_BYTES = 20 * 2**20
XP = 16
LEFT = 8


def gelu_slope(values):
    inner = GELU_SCALE * (values + GELU_CUBIC * values * values * values)
    tangent = jnp.tanh(inner)
    outer = (
        0.5
        * values
        * (1.0 - tangent * tangent)
        * GELU_SCALE
        * (1.0 + 3.0 * GELU_CUBIC * values * values)
    )
    return 0.5 * (1.0 + tangent) + outer


def list_slots(dims, count_of, slot, fields):
    _, slots, heads, cap = dims
    width = slot.shape[0]
    for index in range(slots):
        for field in range(width):
            slot[field, index] = 0

    def head(j, used):
        count = count_of(j)
        for r in range(cap):
            live = (r < count) & (used < slots)

            @pl.when(live)
            def _():
                for field, value in enumerate(fields(j, r)):
                    slot[field, used] = value

            used = used + live.astype(jnp.int32)
        return used

    return lax.fori_loop(0, heads, head, 0)


def crop_kernel(dims, own_ref, row_ref, col_ref, map_ref, below_ref, crop_ref, wide, slot):
    side, slots, _, _ = dims
    high, width, channels = map_ref.shape
    halo = side - 1
    area = side * XP
    used = list_slots(dims, lambda j: own_ref[j], slot, lambda j, r: (row_ref[j, r], col_ref[j, r]))

    wide[pl.ds(0, high), pl.ds(LEFT, width), :] = map_ref[...].astype(F32)
    wide[pl.ds(high, halo), pl.ds(LEFT, width), :] = below_ref[pl.ds(0, halo)].astype(F32)

    columns = lax.broadcasted_iota(jnp.int32, (side, XP, channels), 1)
    for s in range(slots):
        left = slot[1, s]
        base = pl.multiple_of(left // 8 * 8, 8)
        window = wide[pl.ds(slot[0, s], side), pl.ds(base + LEFT, 3 * XP // 2), :]
        window = pltpu.roll(window, lax.rem(3 * XP // 2 - lax.rem(left, 8), 3 * XP // 2), 1)[:, :XP]
        last = jnp.where(s < used, side, 0)
        window = jnp.where(columns < last, window, 0.0).astype(BF16)
        crop_ref[pl.ds(s * area, area), :] = window.reshape(area, channels)


def forward_kernel(dims, me_ref, own_ref, other_ref, weight_ref, gelu_ref, gelu_other_ref, shifted):
    side, slots, _, _ = dims
    channels = own_ref.shape[1]
    half = channels // 2
    area = side * XP
    padded = (side + 2) * XP
    core = lax.rem(me_ref[0], 2)
    lanes = pl.ds(pl.multiple_of(core * half, half), half)

    none = jnp.zeros((XP, channels), BF16)
    for s in range(2 * slots):
        source = own_ref if s < slots else other_ref
        crop = source[pl.ds(s % slots * area, area), :]
        loose = crop.astype(F32)
        for b in range(3):
            moved = crop if b == 1 else pltpu.roll(loose, (area + 1 - b) % area, 0).astype(BF16)
            shifted[b, pl.ds(s * padded, XP), :] = none
            shifted[b, pl.ds(s * padded + XP, area), :] = moved
            shifted[b, pl.ds(s * padded + XP + area, XP), :] = none

    for s in range(2 * slots):
        taps = [
            shifted[b, pl.ds(s * padded + a * XP, area), :] for a in range(3) for b in range(3)
        ]
        lhs = jnp.concatenate(taps, axis=1)
        rows = pl.ds(s % slots * area, area)
        if s < slots:
            matrix = weight_ref[...].reshape(9 * channels, channels)
            gelu_ref[rows, :] = gelu_slope(jnp.dot(lhs, matrix, preferred_element_type=F32))
        else:
            matrix = weight_ref[:, :, lanes].reshape(9 * channels, half)
            gelu_other_ref[rows, :] = gelu_slope(jnp.dot(lhs, matrix, preferred_element_type=F32))


def slope_kernel(dims, me_ref, own_ref, ours_ref, across_ref, gelu_ref, gelu_other_ref, shifted,
                 terms_ref, slope_ref, slid, prior, partner_count, slot, partner_slot, staged, sems):
    side, slots, heads, _ = dims
    boxes = ours_ref.shape[1]
    channels = gelu_ref.shape[1]
    half = channels // 2
    area = side * XP
    padded = (side + 2) * XP
    me = me_ref[0]
    core = lax.rem(me, 2)
    even = me - core
    partner = even + 1 - core
    lanes = pl.ds(pl.multiple_of(core * half, half), half)

    lane = lax.broadcasted_iota(jnp.int32, (8, channels), 1)
    line = lax.broadcasted_iota(jnp.int32, (8, channels), 0)
    totals = jnp.zeros((8, channels), F32)
    counts = jnp.zeros((8, channels), F32)
    for i in range(heads):
        row = jnp.where(core == i % 2, ours_ref[i // 2, 0, 0], across_ref[i // 2, 0, 0]).astype(F32)[8:16]
        totals = totals + jnp.where(i < even, row, 0.0)
        counts = counts + jnp.where(i == partner, row, 0.0)
    totals = jnp.where(line == side - 8, totals, 0.0)
    counts = jnp.where(line == side - 8, counts, 0.0)
    for j in range(heads):
        prior[j] = jnp.sum(jnp.where(lane == j, totals, 0.0)).astype(jnp.int32)
        partner_count[j] = jnp.sum(jnp.where(lane == j, counts, 0.0)).astype(jnp.int32)

    def box(j, r, ahead):
        return j, jnp.minimum(prior[j] + ahead + r, boxes - 1)

    used = list_slots(
        dims, lambda j: own_ref[j], slot, lambda j, r: box(j, r, core * partner_count[j])
    )
    partner_used = list_slots(
        dims, lambda j: partner_count[j], partner_slot, lambda j, r: box(j, r, (1 - core) * own_ref[j])
    )

    def masked(slope, last, width):
        columns = lax.broadcasted_iota(jnp.int32, (side, XP, width), 1).reshape(area, width)
        return jnp.where(columns < last, slope, 0.0).astype(BF16)

    for s in range(2 * slots):
        table, number, count = (slot, s, used) if s < slots else (partner_slot, s - slots, partner_used)
        chip = table[0, number] // 2
        index = table[1, number]
        same = lax.rem(table[0, number], 2) == core
        last = jnp.where(number < count, side, 0)
        rows = pl.ds(number * area, area)
        if s < slots:
            upstream = jnp.where(same, ours_ref[chip, index], across_ref[chip, index]).astype(F32)
            slope = masked(upstream.reshape(area, channels) * gelu_ref[rows, :], last, channels)
            slope_ref[rows, :] = slope
            slope = jnp.where(core == 0, slope[:, :half], slope[:, half:])
        else:
            upstream = jnp.where(
                same, ours_ref[chip, index, :, :, lanes], across_ref[chip, index, :, :, lanes]
            ).astype(F32)
            slope = masked(upstream.reshape(area, half) * gelu_other_ref[rows, :], last, half)
        for a in range(3):
            if a > 0:
                slid[a, pl.ds(s * padded, a * XP), :] = jnp.zeros((a * XP, half), BF16)
            slid[a, pl.ds(s * padded + a * XP, area), :] = slope
            if a < 2:
                slid[a, pl.ds(s * padded + a * XP + area, (2 - a) * XP), :] = jnp.zeros(
                    ((2 - a) * XP, half), BF16
                )

    rhs = jnp.concatenate([slid[a] for a in range(3)], axis=1)
    copies = []
    for b in range(3):
        terms = lax.dot_general(
            shifted[b], rhs, (((0,), (0,)), ((), ())), preferred_element_type=F32
        )
        for a in range(3):
            tap = 3 * a + b
            rows = pl.ds(tap * channels, channels)
            staged[rows, :] = terms[:, a * half : (a + 1) * half].astype(BF16)
            copy = pltpu.make_async_copy(staged.at[rows], terms_ref.at[rows], sems.at[tap])
            copy.start()
            copies.append(copy)
    for copy in copies:
        copy.wait()


def backward_kernel(dims, own_ref, row_ref, col_ref, slope_ref, weight_ref, main_ref, spill_ref, canvas, shifted,
                    slot):
    side, slots, _, _ = dims
    high = main_ref.shape[0]
    width = main_ref.shape[1]
    channels = main_ref.shape[2]
    halo = spill_ref.shape[0]
    area = side * XP

    used = list_slots(dims, lambda j: own_ref[j], slot, lambda j, r: (row_ref[j, r], col_ref[j, r]))
    canvas[...] = jnp.zeros(canvas.shape, F32)
    none = jnp.zeros((XP, channels), BF16)
    rhs = jnp.concatenate([weight_ref[k] for k in range(9)], axis=1)
    columns = lax.broadcasted_iota(jnp.int32, (side, XP, channels), 1)
    for s in range(slots):
        slope = slope_ref[pl.ds(s * area, area), :].astype(F32)
        for b in range(3):
            moved = slope if b == 1 else pltpu.roll(slope, (area + b - 1) % area, 0)
            shifted[b, pl.ds(0, XP), :] = none
            shifted[b, pl.ds(XP, area), :] = moved.astype(BF16)
            shifted[b, pl.ds(XP + area, XP), :] = none
        taps = [shifted[b, pl.ds((2 - a) * XP, area), :] for a in range(3) for b in range(3)]
        lhs = jnp.concatenate(taps, axis=1)
        grad = lax.dot_general(lhs, rhs, (((1,), (1,)), ((), ())), preferred_element_type=F32)
        grad = grad.astype(BF16).astype(F32).reshape(side, XP, channels)
        last = jnp.where(s < used, side, 0)
        grad = jnp.where(columns < last, grad, 0.0)
        left = slot[1, s]
        grad = jnp.concatenate([grad, jnp.zeros((side, XP // 2, channels), F32)], axis=1)
        grad = pltpu.roll(grad, lax.rem(left, 8), 1)
        base = pl.multiple_of(left // 8 * 8, 8)
        place = (pl.ds(slot[0, s], side), pl.ds(base, XP + XP // 2), slice(None))
        canvas[place] = canvas[place] + grad
    main_ref[...] = canvas[pl.ds(0, high), pl.ds(0, width), :]
    spill_ref[...] = canvas[pl.ds(high, halo), pl.ds(0, width), :].astype(spill_ref.dtype)


def merge_kernel(dims, main_ref, arriving_ref, out_ref):
    halo = arriving_ref.shape[0]
    out_ref[pl.ds(0, halo)] = main_ref[pl.ds(0, halo)] + arriving_ref[...].astype(F32)
    out_ref[pl.ds(halo, main_ref.shape[0] - halo)] = main_ref[pl.ds(halo, main_ref.shape[0] - halo)]


def write_half(part, source_ref, out_ref, staged, sems):
    half = source_ref.shape[1]
    pieces = sems.shape[0]
    rows = source_ref.shape[0] // pieces
    lanes = pl.ds(pl.multiple_of(part * half, half), half)
    copies = []
    for piece in range(pieces):
        block = pl.ds(piece * rows, rows)
        staged[block, :] = source_ref[block, :].astype(F32)
        copy = pltpu.make_async_copy(staged.at[block], out_ref.at[block, lanes], sems.at[piece])
        copy.start()
        copies.append(copy)
    for copy in copies:
        copy.wait()


def first_kernel(dims, core_ref, mine_ref, out_ref, staged, sems):
    write_half(core_ref[0], mine_ref, out_ref, staged, sems)


def finish_kernel(dims, core_ref, other_ref, begun_ref, out_ref, staged, sems):
    write_half(1 - core_ref[0], other_ref, out_ref, staged, sems)


def smem():
    return pl.BlockSpec(memory_space=pltpu.SMEM)


def vmem():
    return pl.BlockSpec(memory_space=pltpu.VMEM)


def kernel(body, dims, out_shape, in_specs, scratch_shapes, out_specs=None, aliases=None):
    return pl.pallas_call(
        lambda *refs: body(dims, *refs),
        out_shape=out_shape,
        in_specs=in_specs,
        out_specs=out_specs or jax.tree.map(lambda _: vmem(), out_shape),
        input_output_aliases=aliases or {},
        scratch_shapes=scratch_shapes,
        compiler_params=pltpu.CompilerParams(vmem_limit_bytes=VMEM_BYTES),
    )


def shift(array, axis, by):
    length = lax.axis_size(axis)
    pairs = [(i, i + by) for i in range(length) if 0 <= i + by < length]
    return lax.ppermute(array, axis, pairs)


def repeated(array, times):
    return jnp.broadcast_to(array[None], (times,) + array.shape)


def on_device(feature_map, weight, mask_grad, send_count, send_row, send_col):
    tile_map = feature_map[0]
    high, width, channels = tile_map.shape
    boxes, side = mask_grad.shape[2], mask_grad.shape[3]
    heads, cap = send_row.shape[2], send_row.shape[3]
    owners = lax.axis_size("dp")
    tiles = lax.axis_size("tile")
    slots = boxes * cap
    halo = side - 1
    area, padded = side * XP, (side + 2) * XP
    dims = (side, slots, heads, cap)
    me = lax.axis_index("dp")
    me_array = me.reshape(1).astype(jnp.int32)
    own, top_rows, left_cols = send_count[0, 0], send_row[0, 0], send_col[0, 0]
    partner = [(i, i ^ 1) for i in range(owners)]
    chips = owners // 2
    same_core = [[2 * i + c for i in range(chips)] for c in range(2)]

    half = channels // 2
    core = lax.rem(me, 2)

    below = shift(tile_map, "tile", -1)
    spare = jnp.pad(own.astype(BF16), (0, channels - heads))
    spare = jnp.broadcast_to(spare, (boxes, side, XP - side, channels))
    up = jnp.concatenate([mask_grad[0, 0], spare], 2)
    sent = repeated(up, chips)
    ups = lax.all_to_all(sent, "dp", 0, 0, axis_index_groups=same_core, tiled=True)
    partner_ups = lax.ppermute(ups, "dp", partner)

    crops = kernel(
        crop_kernel,
        dims,
        jax.ShapeDtypeStruct((slots * area, channels), BF16),
        [smem()] * 3 + [vmem()] * 2,
        [
            pltpu.VMEM((high + halo, width + 2 * LEFT, channels), F32),
            pltpu.SMEM((2, slots), jnp.int32),
        ],
    )(own, top_rows, left_cols, tile_map, below)
    partner_crops = lax.ppermute(crops, "dp", partner)

    gelu, gelu_other, shifted = kernel(
        forward_kernel,
        dims,
        (
            pltpu.VMEM((slots * area, channels), F32),
            pltpu.VMEM((slots * area, half), F32),
            pltpu.VMEM((3, 2 * slots * padded, channels), BF16),
        ),
        [smem()] + [vmem()] * 3,
        [],
    )(me_array, crops, partner_crops, weight)

    terms, slope = kernel(
        slope_kernel,
        dims,
        (
            pltpu.HBM((9 * channels, half), BF16),
            jax.ShapeDtypeStruct((slots * area, channels), BF16),
        ),
        [smem()] * 2 + [vmem()] * 5,
        [
            pltpu.VMEM((3, 2 * slots * padded, half), BF16),
            pltpu.SMEM((heads,), jnp.int32),
            pltpu.SMEM((heads,), jnp.int32),
            pltpu.SMEM((2, slots), jnp.int32),
            pltpu.SMEM((2, slots), jnp.int32),
            pltpu.VMEM((9 * channels, half), BF16),
            pltpu.SemaphoreType.DMA((9,)),
        ],
        out_specs=(pl.BlockSpec(memory_space=pltpu.HBM), vmem()),
    )(me_array, own, ups, partner_ups, gelu, gelu_other, shifted)

    main, spill = pl.pallas_call(
        lambda *refs: backward_kernel(dims, *refs),
        out_shape=(
            jax.ShapeDtypeStruct((high, width, channels), F32),
            jax.ShapeDtypeStruct((halo, width, channels), BF16),
        ),
        in_specs=[smem()] * 3 + [vmem()] * 2,
        out_specs=(vmem(), vmem()),
        scratch_shapes=[
            pltpu.VMEM((high + halo, width + XP, channels), F32),
            pltpu.VMEM((3, padded, channels), BF16),
            pltpu.SMEM((2, slots), jnp.int32),
        ],
        name="backward",
        compiler_params=pltpu.CompilerParams(vmem_limit_bytes=VMEM_BYTES),
    )(own, top_rows, left_cols, slope, weight)
    arriving = shift(spill, "tile", 1)
    map_grad = kernel(
        merge_kernel, dims, jax.ShapeDtypeStruct((high, width, channels), F32), [vmem()] * 2, []
    )(main, arriving)

    part = 9 * channels
    deep = 16 if tiles % 16 == 0 else 1
    wide = tiles // deep
    plane = [
        [(x * deep + z) * owners + 2 * y + c for x in range(wide) for y in range(chips)]
        for z in range(deep)
        for c in range(2)
    ]
    stick = [[x * deep + z for z in range(deep)] for x in range(wide)]
    near = wide * chips
    got = lax.all_to_all(
        terms.reshape(near, part // near, half), ("tile", "dp"), 0, 0, axis_index_groups=plane, tiled=True
    )
    column = got.astype(F32).sum(0)
    got = lax.all_to_all(
        column.reshape(deep, part // near // deep, half), "tile", 0, 0, axis_index_groups=stick, tiled=True
    )
    chunk = (got.sum(0) / (boxes * tiles * owners)).astype(BF16)
    got = lax.all_to_all(repeated(chunk, deep), "tile", 0, 0, axis_index_groups=stick, tiled=True)
    got = got.reshape(part // near, half)
    got = lax.all_to_all(repeated(got, near), ("tile", "dp"), 0, 0, axis_index_groups=plane, tiled=True)
    got = got.reshape(part, half)
    other = lax.ppermute(got, "dp", partner)
    whole = pltpu.HBM((part, channels), F32)
    room = [pltpu.VMEM((part, half), F32), pltpu.SemaphoreType.DMA((4,))]
    hbm = pl.BlockSpec(memory_space=pltpu.HBM)
    begun = kernel(first_kernel, dims, whole, [smem(), vmem()], room, hbm)(core.reshape(1), got)
    weight_grad = kernel(
        finish_kernel, dims, whole, [smem(), vmem(), hbm], room, hbm, {2: 0}
    )(core.reshape(1), other, begun)
    return map_grad[None], weight_grad.reshape(9, channels, channels)


def solution(mesh):
    in_specs = (
        P("dp", "tile", None, None),
        P(),
        P("dp", "tile", None, None, None, None),
        P("dp", "tile", None),
        P("dp", "tile", None, None),
        P("dp", "tile", None, None),
    )
    out_specs = (P("dp", "tile", None, None), P())

    return jax.shard_map(on_device, mesh=mesh, in_specs=in_specs, out_specs=out_specs, check_vma=False)
```

```python
import jax
import jax.numpy as jnp
from jax import lax
from jax.experimental import pallas as pl
from jax.experimental.pallas import tpu as pltpu
from jax.sharding import PartitionSpec as P


GELU_SCALE = 0.7978845608
GELU_CUBIC = 0.044715
F32 = jnp.float32
BF16 = jnp.bfloat16
VMEM_BYTES = 20 * 2**20
XP = 16
LEFT = 8


def gelu_slope(values):
    inner = GELU_SCALE * (values + GELU_CUBIC * values * values * values)
    tangent = jnp.tanh(inner)
    outer = (
        0.5
        * values
        * (1.0 - tangent * tangent)
        * GELU_SCALE
        * (1.0 + 3.0 * GELU_CUBIC * values * values)
    )
    return 0.5 * (1.0 + tangent) + outer


def list_slots(dims, count_of, slot, fields):
    _, slots, heads, cap = dims
    width = slot.shape[0]
    for index in range(slots):
        for field in range(width):
            slot[field, index] = 0

    def head(j, used):
        count = count_of(j)
        for r in range(cap):
            live = (r < count) & (used < slots)

            @pl.when(live)
            def _():
                for field, value in enumerate(fields(j, r)):
                    slot[field, used] = value

            used = used + live.astype(jnp.int32)
        return used

    return lax.fori_loop(0, heads, head, 0)


def crop_kernel(dims, own_ref, row_ref, col_ref, map_ref, below_ref, crop_ref, wide, slot):
    side, slots, _, _ = dims
    high, width, channels = map_ref.shape
    halo = side - 1
    area = side * XP
    used = list_slots(dims, lambda j: own_ref[j], slot, lambda j, r: (row_ref[j, r], col_ref[j, r]))

    wide[pl.ds(0, high), pl.ds(LEFT, width), :] = map_ref[...].astype(F32)
    wide[pl.ds(high, halo), pl.ds(LEFT, width), :] = below_ref[pl.ds(0, halo)].astype(F32)

    columns = lax.broadcasted_iota(jnp.int32, (side, XP, channels), 1)
    for s in range(slots):
        left = slot[1, s]
        base = pl.multiple_of(left // 8 * 8, 8)
        window = wide[pl.ds(slot[0, s], side), pl.ds(base + LEFT, 3 * XP // 2), :]
        window = pltpu.roll(window, lax.rem(3 * XP // 2 - lax.rem(left, 8), 3 * XP // 2), 1)[:, :XP]
        last = jnp.where(s < used, side, 0)
        window = jnp.where(columns < last, window, 0.0).astype(BF16)
        crop_ref[pl.ds(s * area, area), :] = window.reshape(area, channels)


def forward_kernel(dims, me_ref, own_ref, other_ref, weight_ref, gelu_ref, shifted):
    side, slots, _, _ = dims
    channels = own_ref.shape[1]
    half = channels // 2
    area = side * XP
    padded = (side + 2) * XP
    core = lax.rem(me_ref[0], 2)
    lanes = pl.ds(pl.multiple_of(core * half, half), half)

    none = jnp.zeros((XP, channels), BF16)
    for s in range(2 * slots):
        source = own_ref if s < slots else other_ref
        crop = source[pl.ds(s % slots * area, area), :]
        loose = crop.astype(F32)
        for b in range(3):
            moved = crop if b == 1 else pltpu.roll(loose, (area + 1 - b) % area, 0).astype(BF16)
            shifted[b, pl.ds(s * padded, XP), :] = none
            shifted[b, pl.ds(s * padded + XP, area), :] = moved
            shifted[b, pl.ds(s * padded + XP + area, XP), :] = none

    matrix = weight_ref[:, :, lanes].reshape(9 * channels, half)
    for s in range(2 * slots):
        taps = [
            shifted[b, pl.ds(s * padded + a * XP, area), :] for a in range(3) for b in range(3)
        ]
        lhs = jnp.concatenate(taps, axis=1)
        gelu_ref[pl.ds(s * area, area), :] = gelu_slope(
            jnp.dot(lhs, matrix, preferred_element_type=F32)
        )


def slope_kernel(dims, me_ref, own_ref, up_ref, gelu_ref, shifted,
                 terms_ref, slope_ref, lent_ref, slid, prior, partner_count, slot, partner_slot, staged, kept, sems):
    side, slots, heads, _ = dims
    boxes = up_ref.shape[1]
    half = gelu_ref.shape[1]
    channels = 2 * half
    area = side * XP
    padded = (side + 2) * XP
    me = me_ref[0]
    core = lax.rem(me, 2)
    even = me - core
    partner = even + 1 - core

    lane = lax.broadcasted_iota(jnp.int32, (8, half), 1)
    line = lax.broadcasted_iota(jnp.int32, (8, half), 0)
    totals = jnp.zeros((8, half), F32)
    counts = jnp.zeros((8, half), F32)
    for i in range(heads):
        row = up_ref[i, 0, 0].astype(F32)[8:16]
        totals = totals + jnp.where(i < even, row, 0.0)
        counts = counts + jnp.where(i == partner, row, 0.0)
    totals = jnp.where(line == side - 8, totals, 0.0)
    counts = jnp.where(line == side - 8, counts, 0.0)
    for j in range(heads):
        prior[j] = jnp.sum(jnp.where(lane == j, totals, 0.0)).astype(jnp.int32)
        partner_count[j] = jnp.sum(jnp.where(lane == j, counts, 0.0)).astype(jnp.int32)

    def box(j, r, ahead):
        return j, jnp.minimum(prior[j] + ahead + r, boxes - 1)

    used = list_slots(
        dims, lambda j: own_ref[j], slot, lambda j, r: box(j, r, core * partner_count[j])
    )
    partner_used = list_slots(
        dims, lambda j: partner_count[j], partner_slot, lambda j, r: box(j, r, (1 - core) * own_ref[j])
    )

    columns = lax.broadcasted_iota(jnp.int32, (side, XP, half), 1).reshape(area, half)
    for s in range(2 * slots):
        table, number, count, ref = (
            (slot, s, used, slope_ref) if s < slots else (partner_slot, s - slots, partner_used, kept)
        )
        head = table[0, number]
        upstream = up_ref[head, table[1, number]].astype(F32)
        last = jnp.where(number < count, side, 0)
        slope = upstream.reshape(area, half) * gelu_ref[pl.ds(s * area, area), :]
        slope = jnp.where(columns < last, slope, 0.0).astype(BF16)
        ref[pl.ds(number * area, area), :] = slope
        for a in range(3):
            if a > 0:
                slid[a, pl.ds(s * padded, a * XP), :] = jnp.zeros((a * XP, half), BF16)
            slid[a, pl.ds(s * padded + a * XP, area), :] = slope
            if a < 2:
                slid[a, pl.ds(s * padded + a * XP + area, (2 - a) * XP), :] = jnp.zeros(
                    ((2 - a) * XP, half), BF16
                )

    rhs = jnp.concatenate([slid[a] for a in range(3)], axis=1)
    copies = [pltpu.make_async_copy(kept, lent_ref, sems.at[9])]
    copies[0].start()
    for b in range(3):
        terms = lax.dot_general(
            shifted[b], rhs, (((0,), (0,)), ((), ())), preferred_element_type=F32
        )
        for a in range(3):
            tap = 3 * a + b
            rows = pl.ds(tap * channels, channels)
            staged[rows, :] = terms[:, a * half : (a + 1) * half].astype(BF16)
            copy = pltpu.make_async_copy(staged.at[rows], terms_ref.at[rows], sems.at[tap])
            copy.start()
            copies.append(copy)
    for copy in copies:
        copy.wait()


def backward_kernel(dims, me_ref, own_ref, row_ref, col_ref, slope_ref, back_ref, weight_ref, main_ref, spill_ref, canvas, shifted,
                    slot):
    side, slots, _, _ = dims
    high = main_ref.shape[0]
    width = main_ref.shape[1]
    channels = main_ref.shape[2]
    halo = spill_ref.shape[0]
    area = side * XP

    used = list_slots(dims, lambda j: own_ref[j], slot, lambda j, r: (row_ref[j, r], col_ref[j, r]))
    core = lax.rem(me_ref[0], 2)
    canvas[...] = jnp.zeros(canvas.shape, F32)
    none = jnp.zeros((XP, channels), BF16)
    rhs = jnp.concatenate([weight_ref[k] for k in range(9)], axis=1)
    columns = lax.broadcasted_iota(jnp.int32, (side, XP, channels), 1)
    for s in range(slots):
        ours = slope_ref[pl.ds(s * area, area), :].astype(F32)
        theirs = back_ref[pl.ds(s * area, area), :].astype(F32)
        slope = jnp.concatenate(
            [jnp.where(core == 0, ours, theirs), jnp.where(core == 0, theirs, ours)], axis=1
        )
        for b in range(3):
            moved = slope if b == 1 else pltpu.roll(slope, (area + b - 1) % area, 0)
            shifted[b, pl.ds(0, XP), :] = none
            shifted[b, pl.ds(XP, area), :] = moved.astype(BF16)
            shifted[b, pl.ds(XP + area, XP), :] = none
        taps = [shifted[b, pl.ds((2 - a) * XP, area), :] for a in range(3) for b in range(3)]
        lhs = jnp.concatenate(taps, axis=1)
        grad = lax.dot_general(lhs, rhs, (((1,), (1,)), ((), ())), preferred_element_type=F32)
        grad = grad.astype(BF16).astype(F32).reshape(side, XP, channels)
        last = jnp.where(s < used, side, 0)
        grad = jnp.where(columns < last, grad, 0.0)
        left = slot[1, s]
        grad = jnp.concatenate([grad, jnp.zeros((side, XP // 2, channels), F32)], axis=1)
        grad = pltpu.roll(grad, lax.rem(left, 8), 1)
        base = pl.multiple_of(left // 8 * 8, 8)
        place = (pl.ds(slot[0, s], side), pl.ds(base, XP + XP // 2), slice(None))
        canvas[place] = canvas[place] + grad
    main_ref[...] = canvas[pl.ds(0, high), pl.ds(0, width), :]
    spill_ref[...] = canvas[pl.ds(high, halo), pl.ds(0, width), :].astype(spill_ref.dtype)


def merge_kernel(dims, main_ref, arriving_ref, out_ref):
    halo = arriving_ref.shape[0]
    out_ref[pl.ds(0, halo)] = main_ref[pl.ds(0, halo)] + arriving_ref[...].astype(F32)
    out_ref[pl.ds(halo, main_ref.shape[0] - halo)] = main_ref[pl.ds(halo, main_ref.shape[0] - halo)]


def write_half(part, source_ref, out_ref, staged, sems):
    half = source_ref.shape[1]
    pieces = sems.shape[0]
    rows = source_ref.shape[0] // pieces
    lanes = pl.ds(pl.multiple_of(part * half, half), half)
    copies = []
    for piece in range(pieces):
        block = pl.ds(piece * rows, rows)
        staged[block, :] = source_ref[block, :].astype(F32)
        copy = pltpu.make_async_copy(staged.at[block], out_ref.at[block, lanes], sems.at[piece])
        copy.start()
        copies.append(copy)
    for copy in copies:
        copy.wait()


def first_kernel(dims, core_ref, mine_ref, out_ref, staged, sems):
    write_half(core_ref[0], mine_ref, out_ref, staged, sems)


def finish_kernel(dims, core_ref, other_ref, begun_ref, out_ref, staged, sems):
    write_half(1 - core_ref[0], other_ref, out_ref, staged, sems)


def smem():
    return pl.BlockSpec(memory_space=pltpu.SMEM)


def vmem():
    return pl.BlockSpec(memory_space=pltpu.VMEM)


def kernel(body, dims, out_shape, in_specs, scratch_shapes, out_specs=None, aliases=None):
    return pl.pallas_call(
        lambda *refs: body(dims, *refs),
        out_shape=out_shape,
        in_specs=in_specs,
        out_specs=out_specs or jax.tree.map(lambda _: vmem(), out_shape),
        input_output_aliases=aliases or {},
        scratch_shapes=scratch_shapes,
        compiler_params=pltpu.CompilerParams(vmem_limit_bytes=VMEM_BYTES),
    )


def shift(array, axis, by):
    length = lax.axis_size(axis)
    pairs = [(i, i + by) for i in range(length) if 0 <= i + by < length]
    return lax.ppermute(array, axis, pairs)


def repeated(array, times):
    return jnp.broadcast_to(array[None], (times,) + array.shape)


def on_device(feature_map, weight, mask_grad, send_count, send_row, send_col):
    tile_map = feature_map[0]
    high, width, channels = tile_map.shape
    boxes, side = mask_grad.shape[2], mask_grad.shape[3]
    heads, cap = send_row.shape[2], send_row.shape[3]
    owners = lax.axis_size("dp")
    tiles = lax.axis_size("tile")
    slots = boxes * cap
    halo = side - 1
    area, padded = side * XP, (side + 2) * XP
    dims = (side, slots, heads, cap)
    me = lax.axis_index("dp")
    me_array = me.reshape(1).astype(jnp.int32)
    own, top_rows, left_cols = send_count[0, 0], send_row[0, 0], send_col[0, 0]
    partner = [(i, i ^ 1) for i in range(owners)]
    chips = owners // 2

    half = channels // 2
    core = lax.rem(me, 2)

    below = shift(tile_map, "tile", -1)
    spare = jnp.pad(own.astype(BF16), (0, half - heads))
    spare = jnp.broadcast_to(spare, (2, boxes, side, XP - side, half))
    halves = mask_grad[0, 0].reshape(boxes, side, side, 2, half).transpose(3, 0, 1, 2, 4)
    sent = repeated(jnp.concatenate([halves, spare], 3), chips)
    sent = sent.reshape((owners,) + sent.shape[2:])
    ups = lax.all_to_all(sent, "dp", 0, 0, tiled=True)

    crops = kernel(
        crop_kernel,
        dims,
        jax.ShapeDtypeStruct((slots * area, channels), BF16),
        [smem()] * 3 + [vmem()] * 2,
        [
            pltpu.VMEM((high + halo, width + 2 * LEFT, channels), F32),
            pltpu.SMEM((2, slots), jnp.int32),
        ],
    )(own, top_rows, left_cols, tile_map, below)
    partner_crops = lax.ppermute(crops, "dp", partner)

    gelu, shifted = kernel(
        forward_kernel,
        dims,
        (
            pltpu.VMEM((2 * slots * area, half), F32),
            pltpu.VMEM((3, 2 * slots * padded, channels), BF16),
        ),
        [smem()] + [vmem()] * 3,
        [],
    )(me_array, crops, partner_crops, weight)

    strip = jax.ShapeDtypeStruct((slots * area, half), BF16)
    terms, slope, lent = kernel(
        slope_kernel,
        dims,
        (pltpu.HBM((9 * channels, half), BF16), strip, pltpu.HBM(strip.shape, BF16)),
        [smem()] * 2 + [vmem()] * 3,
        [
            pltpu.VMEM((3, 2 * slots * padded, half), BF16),
            pltpu.SMEM((heads,), jnp.int32),
            pltpu.SMEM((heads,), jnp.int32),
            pltpu.SMEM((2, slots), jnp.int32),
            pltpu.SMEM((2, slots), jnp.int32),
            pltpu.VMEM((9 * channels, half), BF16),
            pltpu.VMEM((slots * area, half), BF16),
            pltpu.SemaphoreType.DMA((10,)),
        ],
        (pl.BlockSpec(memory_space=pltpu.HBM), vmem(), pl.BlockSpec(memory_space=pltpu.HBM)),
    )(me_array, own, ups, gelu, shifted)
    returned = lax.ppermute(lent, "dp", partner)

    main, spill = kernel(
        backward_kernel,
        dims,
        (
            jax.ShapeDtypeStruct((high, width, channels), F32),
            jax.ShapeDtypeStruct((halo, width, channels), BF16),
        ),
        [smem()] * 4 + [vmem()] * 3,
        [
            pltpu.VMEM((high + halo, width + XP, channels), F32),
            pltpu.VMEM((3, padded, channels), BF16),
            pltpu.SMEM((2, slots), jnp.int32),
        ],
    )(me_array, own, top_rows, left_cols, slope, returned, weight)
    arriving = shift(spill, "tile", 1)
    map_grad = kernel(
        merge_kernel, dims, jax.ShapeDtypeStruct((high, width, channels), F32), [vmem()] * 2, []
    )(main, arriving)

    part = 9 * channels
    deep = 16 if tiles % 16 == 0 else 1
    wide = tiles // deep
    plane = [
        [(x * deep + z) * owners + 2 * y + c for x in range(wide) for y in range(chips)]
        for z in range(deep)
        for c in range(2)
    ]
    stick = [[x * deep + z for z in range(deep)] for x in range(wide)]
    near = wide * chips
    got = lax.all_to_all(
        terms.reshape(near, part // near, half), ("tile", "dp"), 0, 0, axis_index_groups=plane, tiled=True
    )
    column = got.astype(F32).sum(0)
    got = lax.all_to_all(
        column.reshape(deep, part // near // deep, half), "tile", 0, 0, axis_index_groups=stick, tiled=True
    )
    chunk = (got.sum(0) / (boxes * tiles * owners)).astype(BF16)
    got = lax.all_to_all(repeated(chunk, deep), "tile", 0, 0, axis_index_groups=stick, tiled=True)
    got = got.reshape(part // near, half)
    got = lax.all_to_all(repeated(got, near), ("tile", "dp"), 0, 0, axis_index_groups=plane, tiled=True)
    got = got.reshape(part, half)
    other = lax.ppermute(got, "dp", partner)
    whole = pltpu.HBM((part, channels), F32)
    room = [pltpu.VMEM((part, half), F32), pltpu.SemaphoreType.DMA((4,))]
    hbm = pl.BlockSpec(memory_space=pltpu.HBM)
    begun = kernel(first_kernel, dims, whole, [smem(), vmem()], room, hbm)(core.reshape(1), got)
    weight_grad = kernel(
        finish_kernel, dims, whole, [smem(), vmem(), hbm], room, hbm, {2: 0}
    )(core.reshape(1), other, begun)
    return map_grad[None], weight_grad.reshape(9, channels, channels)


def solution(mesh):
    in_specs = (
        P("dp", "tile", None, None),
        P(),
        P("dp", "tile", None, None, None, None),
        P("dp", "tile", None),
        P("dp", "tile", None, None),
        P("dp", "tile", None, None),
    )
    out_specs = (P("dp", "tile", None, None), P())

    return jax.shard_map(on_device, mesh=mesh, in_specs=in_specs, out_specs=out_specs, check_vma=False)
```

```python
import jax
import jax.numpy as jnp
from jax import lax
from jax.experimental import pallas as pl
from jax.experimental.pallas import tpu as pltpu
from jax.sharding import PartitionSpec as P


GELU_SCALE = 0.7978845608
GELU_CUBIC = 0.044715
F32 = jnp.float32
BF16 = jnp.bfloat16
VMEM_BYTES = 20 * 2**20
XP = 16
LEFT = 8


def gelu_slope(values):
    inner = GELU_SCALE * (values + GELU_CUBIC * values * values * values)
    tangent = jnp.tanh(inner)
    outer = (
        0.5
        * values
        * (1.0 - tangent * tangent)
        * GELU_SCALE
        * (1.0 + 3.0 * GELU_CUBIC * values * values)
    )
    return 0.5 * (1.0 + tangent) + outer


def list_slots(dims, count_of, slot, fields):
    _, slots, heads, cap = dims
    width = slot.shape[0]
    for index in range(slots):
        for field in range(width):
            slot[field, index] = 0

    def head(j, used):
        count = count_of(j)
        for r in range(cap):
            live = (r < count) & (used < slots)

            @pl.when(live)
            def _():
                for field, value in enumerate(fields(j, r)):
                    slot[field, used] = value

            used = used + live.astype(jnp.int32)
        return used

    return lax.fori_loop(0, heads, head, 0)


def crop_kernel(dims, own_ref, row_ref, col_ref, map_ref, below_ref, crop_ref, wide, slot):
    side, slots, _, _ = dims
    high, width, channels = map_ref.shape
    halo = side - 1
    area = side * XP
    used = list_slots(dims, lambda j: own_ref[j], slot, lambda j, r: (row_ref[j, r], col_ref[j, r]))

    wide[pl.ds(0, high), pl.ds(LEFT, width), :] = map_ref[...].astype(F32)
    wide[pl.ds(high, halo), pl.ds(LEFT, width), :] = below_ref[pl.ds(0, halo)].astype(F32)

    columns = lax.broadcasted_iota(jnp.int32, (side, XP, channels), 1)
    for s in range(slots):
        left = slot[1, s]
        base = pl.multiple_of(left // 8 * 8, 8)
        window = wide[pl.ds(slot[0, s], side), pl.ds(base + LEFT, 3 * XP // 2), :]
        window = pltpu.roll(window, lax.rem(3 * XP // 2 - lax.rem(left, 8), 3 * XP // 2), 1)[:, :XP]
        last = jnp.where(s < used, side, 0)
        window = jnp.where(columns < last, window, 0.0).astype(BF16)
        crop_ref[pl.ds(s * area, area), :] = window.reshape(area, channels)


def forward_kernel(dims, me_ref, own_ref, other_ref, weight_ref, gelu_ref, shifted):
    side, slots, _, _ = dims
    channels = own_ref.shape[1]
    half = channels // 2
    area = side * XP
    padded = (side + 2) * XP
    core = lax.rem(me_ref[0], 2)
    lanes = pl.ds(pl.multiple_of(core * half, half), half)

    none = jnp.zeros((XP, channels), BF16)
    for s in range(2 * slots):
        source = own_ref if s < slots else other_ref
        crop = source[pl.ds(s % slots * area, area), :]
        loose = crop.astype(F32)
        for b in range(3):
            moved = crop if b == 1 else pltpu.roll(loose, (area + 1 - b) % area, 0).astype(BF16)
            shifted[b, pl.ds(s * padded, XP), :] = none
            shifted[b, pl.ds(s * padded + XP, area), :] = moved
            shifted[b, pl.ds(s * padded + XP + area, XP), :] = none

    matrix = weight_ref[:, :, lanes].reshape(9 * channels, half)
    for s in range(2 * slots):
        taps = [
            shifted[b, pl.ds(s * padded + a * XP, area), :] for a in range(3) for b in range(3)
        ]
        lhs = jnp.concatenate(taps, axis=1)
        gelu_ref[pl.ds(s * area, area), :] = gelu_slope(
            jnp.dot(lhs, matrix, preferred_element_type=F32)
        )


def slope_kernel(dims, me_ref, own_ref, up_ref, gelu_ref, shifted,
                 terms_ref, slope_ref, lent_ref, slid, prior, partner_count, slot, partner_slot, staged, kept, loose, spread, sems):
    side, slots, heads, _ = dims
    boxes = up_ref.shape[1]
    half = gelu_ref.shape[1]
    channels = 2 * half
    area = side * XP
    padded = (side + 2) * XP
    me = me_ref[0]
    core = lax.rem(me, 2)
    even = me - core
    partner = even + 1 - core

    cells = side * side
    tail = cells // 8 * 8
    lane = lax.broadcasted_iota(jnp.int32, (8, half), 1)
    line = lax.broadcasted_iota(jnp.int32, (8, half), 0)
    totals = jnp.zeros((8, half), F32)
    counts = jnp.zeros((8, half), F32)
    for i in range(heads):
        row = up_ref[i, 0].astype(F32)[tail : tail + 8]
        totals = totals + jnp.where(i < even, row, 0.0)
        counts = counts + jnp.where(i == partner, row, 0.0)
    totals = jnp.where(line == cells - tail, totals, 0.0)
    counts = jnp.where(line == cells - tail, counts, 0.0)
    for j in range(heads):
        prior[j] = jnp.sum(jnp.where(lane == j, totals, 0.0)).astype(jnp.int32)
        partner_count[j] = jnp.sum(jnp.where(lane == j, counts, 0.0)).astype(jnp.int32)

    def box(j, r, ahead):
        return j, jnp.minimum(prior[j] + ahead + r, boxes - 1)

    used = list_slots(
        dims, lambda j: own_ref[j], slot, lambda j, r: box(j, r, core * partner_count[j])
    )
    partner_used = list_slots(
        dims, lambda j: partner_count[j], partner_slot, lambda j, r: box(j, r, (1 - core) * own_ref[j])
    )

    columns = lax.broadcasted_iota(jnp.int32, (side, XP, half), 1).reshape(area, half)
    for s in range(2 * slots):
        table, number, count, ref = (
            (slot, s, used, slope_ref) if s < slots else (partner_slot, s - slots, partner_used, kept)
        )
        head = table[0, number]
        loose[s] = up_ref[head, table[1, number]].astype(F32)
        for y in range(side):
            spread[s, pl.ds(y * XP, side), :] = loose[s, pl.ds(y * side, side), :]
        last = jnp.where(number < count, side, 0)
        slope = spread[s] * gelu_ref[pl.ds(s * area, area), :]
        slope = jnp.where(columns < last, slope, 0.0).astype(BF16)
        ref[pl.ds(number * area, area), :] = slope
        for a in range(3):
            if a > 0:
                slid[a, pl.ds(s * padded, a * XP), :] = jnp.zeros((a * XP, half), BF16)
            slid[a, pl.ds(s * padded + a * XP, area), :] = slope
            if a < 2:
                slid[a, pl.ds(s * padded + a * XP + area, (2 - a) * XP), :] = jnp.zeros(
                    ((2 - a) * XP, half), BF16
                )

    rhs = jnp.concatenate([slid[a] for a in range(3)], axis=1)
    copies = [pltpu.make_async_copy(kept, lent_ref, sems.at[9])]
    copies[0].start()
    for b in range(3):
        terms = lax.dot_general(
            shifted[b], rhs, (((0,), (0,)), ((), ())), preferred_element_type=F32
        )
        for a in range(3):
            tap = 3 * a + b
            rows = pl.ds(tap * channels, channels)
            staged[rows, :] = terms[:, a * half : (a + 1) * half].astype(BF16)
            copy = pltpu.make_async_copy(staged.at[rows], terms_ref.at[rows], sems.at[tap])
            copy.start()
            copies.append(copy)
    for copy in copies:
        copy.wait()


def heads_kernel(dims, me_ref, own_ref, crop_ref, other_ref, weight_ref, up_ref,
                 terms_ref, slope_ref, lent_ref, gelu, shifted, *room):
    forward_kernel(dims, me_ref, crop_ref, other_ref, weight_ref, gelu, shifted)
    slope_kernel(dims, me_ref, own_ref, up_ref, gelu, shifted, terms_ref, slope_ref, lent_ref, *room)


def backward_kernel(dims, me_ref, own_ref, row_ref, col_ref, slope_ref, back_ref, weight_ref, main_ref, spill_ref, canvas, shifted,
                    slot):
    side, slots, _, _ = dims
    high = main_ref.shape[0]
    width = main_ref.shape[1]
    channels = main_ref.shape[2]
    halo = spill_ref.shape[0]
    area = side * XP

    used = list_slots(dims, lambda j: own_ref[j], slot, lambda j, r: (row_ref[j, r], col_ref[j, r]))
    core = lax.rem(me_ref[0], 2)
    canvas[...] = jnp.zeros(canvas.shape, F32)
    none = jnp.zeros((XP, channels), BF16)
    rhs = jnp.concatenate([weight_ref[k] for k in range(9)], axis=1)
    columns = lax.broadcasted_iota(jnp.int32, (side, XP, channels), 1)
    for s in range(slots):
        ours = slope_ref[pl.ds(s * area, area), :].astype(F32)
        theirs = back_ref[pl.ds(s * area, area), :].astype(F32)
        slope = jnp.concatenate(
            [jnp.where(core == 0, ours, theirs), jnp.where(core == 0, theirs, ours)], axis=1
        )
        for b in range(3):
            moved = slope if b == 1 else pltpu.roll(slope, (area + b - 1) % area, 0)
            shifted[b, pl.ds(0, XP), :] = none
            shifted[b, pl.ds(XP, area), :] = moved.astype(BF16)
            shifted[b, pl.ds(XP + area, XP), :] = none
        taps = [shifted[b, pl.ds((2 - a) * XP, area), :] for a in range(3) for b in range(3)]
        lhs = jnp.concatenate(taps, axis=1)
        grad = lax.dot_general(lhs, rhs, (((1,), (1,)), ((), ())), preferred_element_type=F32)
        grad = grad.astype(BF16).astype(F32).reshape(side, XP, channels)
        last = jnp.where(s < used, side, 0)
        grad = jnp.where(columns < last, grad, 0.0)
        left = slot[1, s]
        grad = jnp.concatenate([grad, jnp.zeros((side, XP // 2, channels), F32)], axis=1)
        grad = pltpu.roll(grad, lax.rem(left, 8), 1)
        base = pl.multiple_of(left // 8 * 8, 8)
        place = (pl.ds(slot[0, s], side), pl.ds(base, XP + XP // 2), slice(None))
        canvas[place] = canvas[place] + grad
    main_ref[...] = canvas[pl.ds(0, high), pl.ds(0, width), :]
    spill_ref[...] = canvas[pl.ds(high, halo), pl.ds(0, width), :].astype(spill_ref.dtype)


def merge_kernel(dims, main_ref, arriving_ref, out_ref):
    halo = arriving_ref.shape[0]
    out_ref[pl.ds(0, halo)] = main_ref[pl.ds(0, halo)] + arriving_ref[...].astype(F32)
    out_ref[pl.ds(halo, main_ref.shape[0] - halo)] = main_ref[pl.ds(halo, main_ref.shape[0] - halo)]


def write_half(part, source_ref, out_ref, staged, sems):
    half = source_ref.shape[1]
    pieces = sems.shape[0]
    rows = source_ref.shape[0] // pieces
    lanes = pl.ds(pl.multiple_of(part * half, half), half)
    copies = []
    for piece in range(pieces):
        block = pl.ds(piece * rows, rows)
        staged[block, :] = source_ref[block, :].astype(F32)
        copy = pltpu.make_async_copy(staged.at[block], out_ref.at[block, lanes], sems.at[piece])
        copy.start()
        copies.append(copy)
    for copy in copies:
        copy.wait()


def first_kernel(dims, core_ref, mine_ref, out_ref, staged, sems):
    write_half(core_ref[0], mine_ref, out_ref, staged, sems)


def finish_kernel(dims, core_ref, other_ref, begun_ref, out_ref, staged, sems):
    write_half(1 - core_ref[0], other_ref, out_ref, staged, sems)


def smem():
    return pl.BlockSpec(memory_space=pltpu.SMEM)


def vmem():
    return pl.BlockSpec(memory_space=pltpu.VMEM)


def kernel(body, dims, out_shape, in_specs, scratch_shapes, out_specs=None, aliases=None):
    return pl.pallas_call(
        lambda *refs: body(dims, *refs),
        out_shape=out_shape,
        in_specs=in_specs,
        out_specs=out_specs or jax.tree.map(lambda _: vmem(), out_shape),
        input_output_aliases=aliases or {},
        scratch_shapes=scratch_shapes,
        compiler_params=pltpu.CompilerParams(vmem_limit_bytes=VMEM_BYTES),
    )


def shift(array, axis, by):
    length = lax.axis_size(axis)
    pairs = [(i, i + by) for i in range(length) if 0 <= i + by < length]
    return lax.ppermute(array, axis, pairs)


def repeated(array, times):
    return jnp.broadcast_to(array[None], (times,) + array.shape)


def on_device(feature_map, weight, mask_grad, send_count, send_row, send_col):
    tile_map = feature_map[0]
    high, width, channels = tile_map.shape
    boxes, side = mask_grad.shape[2], mask_grad.shape[3]
    heads, cap = send_row.shape[2], send_row.shape[3]
    owners = lax.axis_size("dp")
    tiles = lax.axis_size("tile")
    slots = boxes * cap
    halo = side - 1
    area, padded = side * XP, (side + 2) * XP
    dims = (side, slots, heads, cap)
    me = lax.axis_index("dp")
    me_array = me.reshape(1).astype(jnp.int32)
    own, top_rows, left_cols = send_count[0, 0], send_row[0, 0], send_col[0, 0]
    partner = [(i, i ^ 1) for i in range(owners)]
    chips = owners // 2

    half = channels // 2
    core = lax.rem(me, 2)

    below = shift(tile_map, "tile", -1)
    spare = jnp.pad(own.astype(BF16), (0, half - heads))
    rows = side * side // 8 * 8 + 8
    spare = jnp.broadcast_to(spare, (2, boxes, rows - side * side, half))
    halves = mask_grad[0, 0].reshape(boxes, side * side, 2, half).transpose(2, 0, 1, 3)
    sent = repeated(jnp.concatenate([halves, spare], 2), chips)
    sent = sent.reshape((owners,) + sent.shape[2:])
    ups = lax.all_to_all(sent, "dp", 0, 0, tiled=True)

    crops = kernel(
        crop_kernel,
        dims,
        jax.ShapeDtypeStruct((slots * area, channels), BF16),
        [smem()] * 3 + [vmem()] * 2,
        [
            pltpu.VMEM((high + halo, width + 2 * LEFT, channels), F32),
            pltpu.SMEM((2, slots), jnp.int32),
        ],
    )(own, top_rows, left_cols, tile_map, below)
    partner_crops = lax.ppermute(crops, "dp", partner)

    strip = (slots * area, half)
    hbm = pl.BlockSpec(memory_space=pltpu.HBM)
    terms, slope, lent = kernel(
        heads_kernel,
        dims,
        (pltpu.HBM((9 * channels, half), BF16), jax.ShapeDtypeStruct(strip, BF16), pltpu.HBM(strip, BF16)),
        [smem()] * 2 + [vmem()] * 4,
        [
            pltpu.VMEM((2 * slots * area, half), F32),
            pltpu.VMEM((3, 2 * slots * padded, channels), BF16),
            pltpu.VMEM((3, 2 * slots * padded, half), BF16),
            pltpu.SMEM((heads,), jnp.int32),
            pltpu.SMEM((heads,), jnp.int32),
            pltpu.SMEM((2, slots), jnp.int32),
            pltpu.SMEM((2, slots), jnp.int32),
            pltpu.VMEM((9 * channels, half), BF16),
            pltpu.VMEM(strip, BF16),
            pltpu.VMEM((2 * slots, rows, half), F32),
            pltpu.VMEM((2 * slots, area, half), F32),
            pltpu.SemaphoreType.DMA((10,)),
        ],
        (hbm, vmem(), hbm),
    )(me_array, own, crops, partner_crops, weight, ups)
    returned = lax.ppermute(lent, "dp", partner)

    main, spill = kernel(
        backward_kernel,
        dims,
        (
            jax.ShapeDtypeStruct((high, width, channels), F32),
            jax.ShapeDtypeStruct((halo, width, channels), BF16),
        ),
        [smem()] * 4 + [vmem()] * 3,
        [
            pltpu.VMEM((high + halo, width + XP, channels), F32),
            pltpu.VMEM((3, padded, channels), BF16),
            pltpu.SMEM((2, slots), jnp.int32),
        ],
    )(me_array, own, top_rows, left_cols, slope, returned, weight)
    arriving = shift(spill, "tile", 1)
    map_grad = kernel(
        merge_kernel, dims, jax.ShapeDtypeStruct((high, width, channels), F32), [vmem()] * 2, []
    )(main, arriving)

    part = 9 * channels
    deep = 16 if tiles % 16 == 0 else 1
    wide = tiles // deep
    plane = [
        [(x * deep + z) * owners + 2 * y + c for x in range(wide) for y in range(chips)]
        for z in range(deep)
        for c in range(2)
    ]
    stick = [[x * deep + z for z in range(deep)] for x in range(wide)]
    near = wide * chips
    got = lax.all_to_all(
        terms.reshape(near, part // near, half), ("tile", "dp"), 0, 0, axis_index_groups=plane, tiled=True
    )
    column = got.astype(F32).sum(0)
    got = lax.all_to_all(
        column.reshape(deep, part // near // deep, half), "tile", 0, 0, axis_index_groups=stick, tiled=True
    )
    chunk = (got.sum(0) / (boxes * tiles * owners)).astype(BF16)
    got = lax.all_to_all(repeated(chunk, deep), "tile", 0, 0, axis_index_groups=stick, tiled=True)
    got = got.reshape(part // near, half)
    got = lax.all_to_all(repeated(got, near), ("tile", "dp"), 0, 0, axis_index_groups=plane, tiled=True)
    got = got.reshape(part, half)
    other = lax.ppermute(got, "dp", partner)
    whole = pltpu.HBM((part, channels), F32)
    room = [pltpu.VMEM((part, half), F32), pltpu.SemaphoreType.DMA((4,))]
    begun = kernel(first_kernel, dims, whole, [smem(), vmem()], room, hbm)(core.reshape(1), got)
    weight_grad = kernel(
        finish_kernel, dims, whole, [smem(), vmem(), hbm], room, hbm, {2: 0}
    )(core.reshape(1), other, begun)
    return map_grad[None], weight_grad.reshape(9, channels, channels)


def solution(mesh):
    in_specs = (
        P("dp", "tile", None, None),
        P(),
        P("dp", "tile", None, None, None, None),
        P("dp", "tile", None),
        P("dp", "tile", None, None),
        P("dp", "tile", None, None),
    )
    out_specs = (P("dp", "tile", None, None), P())

    return jax.shard_map(on_device, mesh=mesh, in_specs=in_specs, out_specs=out_specs, check_vma=False)
```

```python
import jax
import jax.numpy as jnp
from jax import lax
from jax.experimental import pallas as pl
from jax.experimental.pallas import tpu as pltpu
from jax.sharding import PartitionSpec as P


GELU_SCALE = 0.7978845608
GELU_CUBIC = 0.044715
F32 = jnp.float32
BF16 = jnp.bfloat16
VMEM_BYTES = 20 * 2**20
XP = 16
LEFT = 8


def gelu_slope(values):
    inner = GELU_SCALE * (values + GELU_CUBIC * values * values * values)
    tangent = jnp.tanh(inner)
    outer = (
        0.5
        * values
        * (1.0 - tangent * tangent)
        * GELU_SCALE
        * (1.0 + 3.0 * GELU_CUBIC * values * values)
    )
    return 0.5 * (1.0 + tangent) + outer


def list_slots(dims, count_of, slot, fields):
    _, slots, heads, cap = dims
    width = slot.shape[0]
    for index in range(slots):
        for field in range(width):
            slot[field, index] = 0

    def head(j, used):
        count = count_of(j)
        for r in range(cap):
            live = (r < count) & (used < slots)

            @pl.when(live)
            def _():
                for field, value in enumerate(fields(j, r)):
                    slot[field, used] = value

            used = used + live.astype(jnp.int32)
        return used

    return lax.fori_loop(0, heads, head, 0)


def pack_kernel(dims, own_ref, mask_ref, sent_ref, loose, staged, sems):
    heads = dims[2]
    boxes, cells, channels = mask_ref.shape
    half = channels // 2
    spare = loose.shape[2] - cells
    lane = lax.broadcasted_iota(jnp.int32, (spare, half), 1)
    counts = jnp.zeros((spare, half), jnp.int32)
    for j in range(heads):
        counts = jnp.where(lane == j, own_ref[j], counts)
    for part in range(2):
        for b in range(boxes):
            loose[part, b, pl.ds(0, cells)] = mask_ref[b, :, part * half : (part + 1) * half].astype(F32)
            loose[part, b, pl.ds(cells, spare)] = counts.astype(F32)
            staged[part, b] = loose[part, b].astype(BF16)
    copies = [
        pltpu.make_async_copy(staged, sent_ref.at[chip], sems.at[chip])
        for chip in range(sent_ref.shape[0])
    ]
    for copy in copies:
        copy.start()
    for copy in copies:
        copy.wait()


def crop_kernel(dims, own_ref, row_ref, col_ref, map_ref, below_ref, crop_ref, wide, slot):
    side, slots, _, _ = dims
    high, width, channels = map_ref.shape
    halo = side - 1
    area = side * XP
    used = list_slots(dims, lambda j: own_ref[j], slot, lambda j, r: (row_ref[j, r], col_ref[j, r]))

    wide[pl.ds(0, high), pl.ds(LEFT, width), :] = map_ref[...].astype(F32)
    wide[pl.ds(high, halo), pl.ds(LEFT, width), :] = below_ref[pl.ds(0, halo)].astype(F32)

    columns = lax.broadcasted_iota(jnp.int32, (side, XP, channels), 1)
    for s in range(slots):
        left = slot[1, s]
        base = pl.multiple_of(left // 8 * 8, 8)
        window = wide[pl.ds(slot[0, s], side), pl.ds(base + LEFT, 3 * XP // 2), :]
        window = pltpu.roll(window, lax.rem(3 * XP // 2 - lax.rem(left, 8), 3 * XP // 2), 1)[:, :XP]
        last = jnp.where(s < used, side, 0)
        window = jnp.where(columns < last, window, 0.0).astype(BF16)
        crop_ref[pl.ds(s * area, area), :] = window.reshape(area, channels)


def forward_kernel(dims, me_ref, own_ref, other_ref, weight_ref, gelu_ref, shifted):
    side, slots, _, _ = dims
    channels = own_ref.shape[1]
    half = channels // 2
    area = side * XP
    padded = (side + 2) * XP
    core = lax.rem(me_ref[0], 2)
    lanes = pl.ds(pl.multiple_of(core * half, half), half)

    none = jnp.zeros((XP, channels), BF16)
    for s in range(2 * slots):
        source = own_ref if s < slots else other_ref
        crop = source[pl.ds(s % slots * area, area), :]
        loose = crop.astype(F32)
        for b in range(3):
            moved = crop if b == 1 else pltpu.roll(loose, (area + 1 - b) % area, 0).astype(BF16)
            shifted[b, pl.ds(s * padded, XP), :] = none
            shifted[b, pl.ds(s * padded + XP, area), :] = moved
            shifted[b, pl.ds(s * padded + XP + area, XP), :] = none

    matrix = weight_ref[:, :, lanes].reshape(9 * channels, half)
    for s in range(2 * slots):
        taps = [
            shifted[b, pl.ds(s * padded + a * XP, area), :] for a in range(3) for b in range(3)
        ]
        lhs = jnp.concatenate(taps, axis=1)
        gelu_ref[pl.ds(s * area, area), :] = gelu_slope(
            jnp.dot(lhs, matrix, preferred_element_type=F32)
        )


def slope_kernel(dims, me_ref, own_ref, up_ref, gelu_ref, shifted,
                 terms_ref, slope_ref, lent_ref, slid, prior, partner_count, slot, partner_slot, staged, kept, loose, spread, sems):
    side, slots, heads, _ = dims
    boxes = up_ref.shape[1]
    half = gelu_ref.shape[1]
    channels = 2 * half
    area = side * XP
    padded = (side + 2) * XP
    me = me_ref[0]
    core = lax.rem(me, 2)
    even = me - core
    partner = even + 1 - core

    cells = side * side
    tail = cells // 8 * 8
    lane = lax.broadcasted_iota(jnp.int32, (8, half), 1)
    line = lax.broadcasted_iota(jnp.int32, (8, half), 0)
    totals = jnp.zeros((8, half), F32)
    counts = jnp.zeros((8, half), F32)
    for i in range(heads):
        row = up_ref[i, 0].astype(F32)[tail : tail + 8]
        totals = totals + jnp.where(i < even, row, 0.0)
        counts = counts + jnp.where(i == partner, row, 0.0)
    totals = jnp.where(line == cells - tail, totals, 0.0)
    counts = jnp.where(line == cells - tail, counts, 0.0)
    for j in range(heads):
        prior[j] = jnp.sum(jnp.where(lane == j, totals, 0.0)).astype(jnp.int32)
        partner_count[j] = jnp.sum(jnp.where(lane == j, counts, 0.0)).astype(jnp.int32)

    def box(j, r, ahead):
        return j, jnp.minimum(prior[j] + ahead + r, boxes - 1)

    used = list_slots(
        dims, lambda j: own_ref[j], slot, lambda j, r: box(j, r, core * partner_count[j])
    )
    partner_used = list_slots(
        dims, lambda j: partner_count[j], partner_slot, lambda j, r: box(j, r, (1 - core) * own_ref[j])
    )

    columns = lax.broadcasted_iota(jnp.int32, (side, XP, half), 1).reshape(area, half)
    for s in range(2 * slots):
        table, number, count, ref = (
            (slot, s, used, slope_ref) if s < slots else (partner_slot, s - slots, partner_used, kept)
        )
        head = table[0, number]
        loose[s] = up_ref[head, table[1, number]].astype(F32)
        for y in range(side):
            spread[s, pl.ds(y * XP, side), :] = loose[s, pl.ds(y * side, side), :]
        last = jnp.where(number < count, side, 0)
        slope = spread[s] * gelu_ref[pl.ds(s * area, area), :]
        slope = jnp.where(columns < last, slope, 0.0).astype(BF16)
        ref[pl.ds(number * area, area), :] = slope
        for a in range(3):
            if a > 0:
                slid[a, pl.ds(s * padded, a * XP), :] = jnp.zeros((a * XP, half), BF16)
            slid[a, pl.ds(s * padded + a * XP, area), :] = slope
            if a < 2:
                slid[a, pl.ds(s * padded + a * XP + area, (2 - a) * XP), :] = jnp.zeros(
                    ((2 - a) * XP, half), BF16
                )

    rhs = jnp.concatenate([slid[a] for a in range(3)], axis=1)
    copies = [pltpu.make_async_copy(kept, lent_ref, sems.at[9])]
    copies[0].start()
    for b in range(3):
        terms = lax.dot_general(
            shifted[b], rhs, (((0,), (0,)), ((), ())), preferred_element_type=F32
        )
        for a in range(3):
            tap = 3 * a + b
            rows = pl.ds(tap * channels, channels)
            staged[rows, :] = terms[:, a * half : (a + 1) * half].astype(BF16)
            copy = pltpu.make_async_copy(staged.at[rows], terms_ref.at[rows], sems.at[tap])
            copy.start()
            copies.append(copy)
    for copy in copies:
        copy.wait()


def heads_kernel(dims, me_ref, own_ref, crop_ref, other_ref, weight_ref, up_ref,
                 terms_ref, slope_ref, lent_ref, gelu, shifted, *room):
    forward_kernel(dims, me_ref, crop_ref, other_ref, weight_ref, gelu, shifted)
    slope_kernel(dims, me_ref, own_ref, up_ref, gelu, shifted, terms_ref, slope_ref, lent_ref, *room)


def backward_kernel(dims, me_ref, own_ref, row_ref, col_ref, slope_ref, back_ref, weight_ref, main_ref, spill_ref, canvas, shifted,
                    slot):
    side, slots, _, _ = dims
    high = main_ref.shape[0]
    width = main_ref.shape[1]
    channels = main_ref.shape[2]
    halo = spill_ref.shape[0]
    area = side * XP

    used = list_slots(dims, lambda j: own_ref[j], slot, lambda j, r: (row_ref[j, r], col_ref[j, r]))
    core = lax.rem(me_ref[0], 2)
    canvas[...] = jnp.zeros(canvas.shape, F32)
    none = jnp.zeros((XP, channels), BF16)
    rhs = jnp.concatenate([weight_ref[k] for k in range(9)], axis=1)
    columns = lax.broadcasted_iota(jnp.int32, (side, XP, channels), 1)
    for s in range(slots):
        ours = slope_ref[pl.ds(s * area, area), :].astype(F32)
        theirs = back_ref[pl.ds(s * area, area), :].astype(F32)
        slope = jnp.concatenate(
            [jnp.where(core == 0, ours, theirs), jnp.where(core == 0, theirs, ours)], axis=1
        )
        for b in range(3):
            moved = slope if b == 1 else pltpu.roll(slope, (area + b - 1) % area, 0)
            shifted[b, pl.ds(0, XP), :] = none
            shifted[b, pl.ds(XP, area), :] = moved.astype(BF16)
            shifted[b, pl.ds(XP + area, XP), :] = none
        taps = [shifted[b, pl.ds((2 - a) * XP, area), :] for a in range(3) for b in range(3)]
        lhs = jnp.concatenate(taps, axis=1)
        grad = lax.dot_general(lhs, rhs, (((1,), (1,)), ((), ())), preferred_element_type=F32)
        grad = grad.astype(BF16).astype(F32).reshape(side, XP, channels)
        last = jnp.where(s < used, side, 0)
        grad = jnp.where(columns < last, grad, 0.0)
        left = slot[1, s]
        grad = jnp.concatenate([grad, jnp.zeros((side, XP // 2, channels), F32)], axis=1)
        grad = pltpu.roll(grad, lax.rem(left, 8), 1)
        base = pl.multiple_of(left // 8 * 8, 8)
        place = (pl.ds(slot[0, s], side), pl.ds(base, XP + XP // 2), slice(None))
        canvas[place] = canvas[place] + grad
    main_ref[...] = canvas[pl.ds(0, high), pl.ds(0, width), :]
    spill_ref[...] = canvas[pl.ds(high, halo), pl.ds(0, width), :].astype(spill_ref.dtype)


def merge_kernel(dims, main_ref, arriving_ref, out_ref):
    halo = arriving_ref.shape[0]
    out_ref[pl.ds(0, halo)] = main_ref[pl.ds(0, halo)] + arriving_ref[...].astype(F32)
    out_ref[pl.ds(halo, main_ref.shape[0] - halo)] = main_ref[pl.ds(halo, main_ref.shape[0] - halo)]


def write_half(part, source_ref, out_ref, staged, sems):
    half = source_ref.shape[1]
    pieces = sems.shape[0]
    rows = source_ref.shape[0] // pieces
    lanes = pl.ds(pl.multiple_of(part * half, half), half)
    copies = []
    for piece in range(pieces):
        block = pl.ds(piece * rows, rows)
        staged[block, :] = source_ref[block, :].astype(F32)
        copy = pltpu.make_async_copy(staged.at[block], out_ref.at[block, lanes], sems.at[piece])
        copy.start()
        copies.append(copy)
    for copy in copies:
        copy.wait()


def first_kernel(dims, core_ref, mine_ref, out_ref, staged, sems):
    write_half(core_ref[0], mine_ref, out_ref, staged, sems)


def finish_kernel(dims, core_ref, other_ref, begun_ref, out_ref, staged, sems):
    write_half(1 - core_ref[0], other_ref, out_ref, staged, sems)


def smem():
    return pl.BlockSpec(memory_space=pltpu.SMEM)


def vmem():
    return pl.BlockSpec(memory_space=pltpu.VMEM)


def kernel(body, dims, out_shape, in_specs, scratch_shapes, out_specs=None, aliases=None):
    return pl.pallas_call(
        lambda *refs: body(dims, *refs),
        out_shape=out_shape,
        in_specs=in_specs,
        out_specs=out_specs or jax.tree.map(lambda _: vmem(), out_shape),
        input_output_aliases=aliases or {},
        scratch_shapes=scratch_shapes,
        compiler_params=pltpu.CompilerParams(vmem_limit_bytes=VMEM_BYTES),
    )


def shift(array, axis, by):
    length = lax.axis_size(axis)
    pairs = [(i, i + by) for i in range(length) if 0 <= i + by < length]
    return lax.ppermute(array, axis, pairs)


def repeated(array, times):
    return jnp.broadcast_to(array[None], (times,) + array.shape)


def on_device(feature_map, weight, mask_grad, send_count, send_row, send_col):
    tile_map = feature_map[0]
    high, width, channels = tile_map.shape
    boxes, side = mask_grad.shape[2], mask_grad.shape[3]
    heads, cap = send_row.shape[2], send_row.shape[3]
    owners = lax.axis_size("dp")
    tiles = lax.axis_size("tile")
    slots = boxes * cap
    halo = side - 1
    area, padded = side * XP, (side + 2) * XP
    dims = (side, slots, heads, cap)
    me = lax.axis_index("dp")
    me_array = me.reshape(1).astype(jnp.int32)
    own, top_rows, left_cols = send_count[0, 0], send_row[0, 0], send_col[0, 0]
    partner = [(i, i ^ 1) for i in range(owners)]
    chips = owners // 2

    half = channels // 2
    core = lax.rem(me, 2)

    below = shift(tile_map, "tile", -1)
    rows = side * side // 8 * 8 + 8
    sent = kernel(
        pack_kernel,
        dims,
        pltpu.HBM((chips, 2, boxes, rows, half), BF16),
        [smem(), vmem()],
        [
            pltpu.VMEM((2, boxes, rows, half), F32),
            pltpu.VMEM((2, boxes, rows, half), BF16),
            pltpu.SemaphoreType.DMA((chips,)),
        ],
        pl.BlockSpec(memory_space=pltpu.HBM),
    )(own, mask_grad[0, 0].reshape(boxes, side * side, channels))
    sent = sent.reshape((owners,) + sent.shape[2:])
    ups = lax.all_to_all(sent, "dp", 0, 0, tiled=True)

    crops = kernel(
        crop_kernel,
        dims,
        jax.ShapeDtypeStruct((slots * area, channels), BF16),
        [smem()] * 3 + [vmem()] * 2,
        [
            pltpu.VMEM((high + halo, width + 2 * LEFT, channels), F32),
            pltpu.SMEM((2, slots), jnp.int32),
        ],
    )(own, top_rows, left_cols, tile_map, below)
    partner_crops = lax.ppermute(crops, "dp", partner)

    strip = (slots * area, half)
    hbm = pl.BlockSpec(memory_space=pltpu.HBM)
    terms, slope, lent = kernel(
        heads_kernel,
        dims,
        (pltpu.HBM((9 * channels, half), BF16), jax.ShapeDtypeStruct(strip, BF16), pltpu.HBM(strip, BF16)),
        [smem()] * 2 + [vmem()] * 4,
        [
            pltpu.VMEM((2 * slots * area, half), F32),
            pltpu.VMEM((3, 2 * slots * padded, channels), BF16),
            pltpu.VMEM((3, 2 * slots * padded, half), BF16),
            pltpu.SMEM((heads,), jnp.int32),
            pltpu.SMEM((heads,), jnp.int32),
            pltpu.SMEM((2, slots), jnp.int32),
            pltpu.SMEM((2, slots), jnp.int32),
            pltpu.VMEM((9 * channels, half), BF16),
            pltpu.VMEM(strip, BF16),
            pltpu.VMEM((2 * slots, rows, half), F32),
            pltpu.VMEM((2 * slots, area, half), F32),
            pltpu.SemaphoreType.DMA((10,)),
        ],
        (hbm, vmem(), hbm),
    )(me_array, own, crops, partner_crops, weight, ups)
    returned = lax.ppermute(lent, "dp", partner)

    main, spill = kernel(
        backward_kernel,
        dims,
        (
            jax.ShapeDtypeStruct((high, width, channels), F32),
            jax.ShapeDtypeStruct((halo, width, channels), BF16),
        ),
        [smem()] * 4 + [vmem()] * 3,
        [
            pltpu.VMEM((high + halo, width + XP, channels), F32),
            pltpu.VMEM((3, padded, channels), BF16),
            pltpu.SMEM((2, slots), jnp.int32),
        ],
    )(me_array, own, top_rows, left_cols, slope, returned, weight)
    arriving = shift(spill, "tile", 1)
    map_grad = kernel(
        merge_kernel, dims, jax.ShapeDtypeStruct((high, width, channels), F32), [vmem()] * 2, []
    )(main, arriving)

    part = 9 * channels
    deep = 16 if tiles % 16 == 0 else 1
    wide = tiles // deep
    plane = [
        [(x * deep + z) * owners + 2 * y + c for x in range(wide) for y in range(chips)]
        for z in range(deep)
        for c in range(2)
    ]
    stick = [[x * deep + z for z in range(deep)] for x in range(wide)]
    near = wide * chips
    got = lax.all_to_all(
        terms.reshape(near, part // near, half), ("tile", "dp"), 0, 0, axis_index_groups=plane, tiled=True
    )
    column = got.astype(F32).sum(0)
    got = lax.all_to_all(
        column.reshape(deep, part // near // deep, half), "tile", 0, 0, axis_index_groups=stick, tiled=True
    )
    chunk = (got.sum(0) / (boxes * tiles * owners)).astype(BF16)
    got = lax.all_to_all(repeated(chunk, deep), "tile", 0, 0, axis_index_groups=stick, tiled=True)
    got = got.reshape(part // near, half)
    got = lax.all_to_all(repeated(got, near), ("tile", "dp"), 0, 0, axis_index_groups=plane, tiled=True)
    got = got.reshape(part, half)
    other = lax.ppermute(got, "dp", partner)
    whole = pltpu.HBM((part, channels), F32)
    room = [pltpu.VMEM((part, half), F32), pltpu.SemaphoreType.DMA((4,))]
    begun = kernel(first_kernel, dims, whole, [smem(), vmem()], room, hbm)(core.reshape(1), got)
    weight_grad = kernel(
        finish_kernel, dims, whole, [smem(), vmem(), hbm], room, hbm, {2: 0}
    )(core.reshape(1), other, begun)
    return map_grad[None], weight_grad.reshape(9, channels, channels)


def solution(mesh):
    in_specs = (
        P("dp", "tile", None, None),
        P(),
        P("dp", "tile", None, None, None, None),
        P("dp", "tile", None),
        P("dp", "tile", None, None),
        P("dp", "tile", None, None),
    )
    out_specs = (P("dp", "tile", None, None), P())

    return jax.shard_map(on_device, mesh=mesh, in_specs=in_specs, out_specs=out_specs, check_vma=False)
```
